32 devices in a mesh: leaf: 8 (over z, x), sub: 4 (over y, core).
Axes of the slice: x: 2, y: 2, z: 4, core: 2. Of those that a mesh axis runs over, the one named last changes fastest.
Arguments:
- points: float32 [65536, 64], P(('leaf', 'sub')), may hold values from -6 to 6
- leaf_maps: float32 [128, 128, 512], P(('leaf', 'sub')), may hold values from -0.25 to 0.25
- root_maps: float32 [128, 128, 512], P(('leaf', 'sub')), may hold values from -0.25 to 0.25
- current: float32 [65536], P(('leaf', 'sub')), may hold values from -6 to 6
- krylov_basis: float32 [8, 65536], P(None, ('leaf', 'sub')), may hold values from -0.0234375 to 0.0234375
- ritz_roots: float32 [2], replicated, may hold values from 40 to 400
- point_order: int32 [65536], P(('leaf', 'sub')), may hold values from 0 to 8191, as said below
- skeleton: int32 [128, 128], P(('leaf', 'sub')), may hold values from 0 to 511, as said below
- root_skeleton: int32 [8, 128], P('leaf'), may hold values from 0 to 8191, as said below
- near_list: int32 [128, 32], P(('leaf', 'sub')), may hold values from 0 to 47, as said below
- far_list: int32 [128, 4], P(('leaf', 'sub')), may hold values from 0 to 47, as said below
Outputs:
- orthogonal: float32 [65536], P(('leaf', 'sub'))
- hessenberg: float32 [9], replicated
The draws below stay inside these ranges and needn't reach their ends.
Inputs may be any that keep to these rules, and one draw needn't show every extreme that they name: Within each subtree (block of 8192 tree positions) point_order is a permutation of 0 to 8191. `skeleton`: each row holds 128 different point numbers of the leaf. `root_skeleton`: each row holds 128 different point numbers of the subtree. `near_list`: slots count 16 leaves of the previous subtree, then the own subtree, then the next one (circularly). The first slot of leaf a is its own, 16 + (a mod 16); the slots of a row are different, and no slot of a row is in the leaf's far_list. `far_list`: slots as in near_list; different within a row, never the leaf's own.
All inputs are finite; a program needn't handle non-finite values.
Results may differ from the reference program's by a relative error of at most 0.000096.
Values sent between devices are 32-bit elements; how exact they have to be, the bound alone decides.
A program may use at most 64 MiB of HBM per device.

```python
import math
import jax
import jax.numpy as jnp
from jax import lax

F = 64
LS = 512
SK = 128
NEAR = 32
FAR = 4
MB = 8
SUBLEAVES = 16
SUBTREES = 8
LEAVES = 128
NPTS = 65536


def slot_tables(key):
    base = jax.random.fold_in(key, 11)
    keys = jax.random.split(base, LEAVES)
    others = jax.vmap(lambda leafkey: jax.random.permutation(leafkey, 3 * SUBLEAVES - 1))(keys).astype(jnp.int32)
    own_slot = (SUBLEAVES + jnp.arange(LEAVES, dtype=jnp.int32) % SUBLEAVES)[:, None].astype(jnp.int32)
    shifted = jnp.where(others >= own_slot, others + 1, others).astype(jnp.int32)
    return (own_slot, shifted)


def draw_near_list(key, part):
    own_slot, shifted = slot_tables(key)
    return jnp.concatenate([own_slot, shifted[:, :NEAR - 1]], axis=1).astype(jnp.int32)


def draw_far_list(key, part):
    own_slot, shifted = slot_tables(key)
    return shifted[:, NEAR - 1:NEAR - 1 + FAR].astype(jnp.int32)


def draw_point_order(key, part):
    keys = jax.random.split(jax.random.fold_in(key, 23), SUBTREES)
    table = jax.vmap(lambda subkey: jax.random.permutation(subkey, SUBLEAVES * LS))(keys)
    return table.reshape(-1).astype(jnp.int32)


def draw_skeleton(key, part):
    keys = jax.random.split(jax.random.fold_in(key, 37), LEAVES)
    table = jax.vmap(lambda leafkey: jax.random.permutation(leafkey, LS)[:SK])(keys)
    return table.astype(jnp.int32)


def draw_root_skeleton(key, part):
    keys = jax.random.split(jax.random.fold_in(key, 41), SUBTREES)
    table = jax.vmap(lambda subkey: jax.random.permutation(subkey, SUBLEAVES * LS)[:SK])(keys)
    return table.astype(jnp.int32)


def levels(stream_key, dims, pieces, smallest, high):
    def one(axis_at, parts):
        heights = jax.random.uniform(jax.random.fold_in(jax.random.fold_in(stream_key, 6), axis_at), (parts,), jnp.float32, smallest / len(pieces), high / len(pieces))
        return jnp.repeat(jnp.exp(heights), dims[axis_at] // parts).reshape((-1,) + (1,) * (len(dims) - axis_at - 1))

    loudness = one(*pieces[0])
    for cut in pieces[1:]:
        loudness = loudness * one(*cut)
    return loudness


def scatter_about(own_key, extent, width, bound, shards=(), kind=jnp.bfloat16):
    values = width * jax.random.normal(own_key, extent, jnp.float32)
    if shards:
        values = values * levels(own_key, extent, shards, -0.22, 0.18)
    return jnp.clip(values, -bound, bound).astype(kind)


def setup_inputs(seed: int = 0) -> dict:
    streams_of = jax.random.split(jax.random.key(seed), 12)
    return {
        "points": scatter_about(streams_of[0], (NPTS, F), 1.0, 6.0, ((0, 32),), jnp.float32),
        "leaf_maps": scatter_about(streams_of[1], (LEAVES, SK, LS), LS ** -0.5, 0.25, ((0, 32),), jnp.float32),
        "root_maps": scatter_about(streams_of[2], (LEAVES, SK, LS), LS ** -0.5, 0.25, ((0, 32),), jnp.float32),
        "current": scatter_about(streams_of[3], (NPTS,), 1.0, 6.0, ((0, 32),), jnp.float32),
        "krylov_basis": scatter_about(streams_of[4], (MB, NPTS), NPTS ** -0.5, 0.0234375, ((1, 32),), jnp.float32),
        "ritz_roots": jnp.clip(jnp.exp(jax.random.uniform(streams_of[5], (2,), jnp.float32, math.log(40.0), math.log(400.0))), 40.0, 400.0),
        "point_order": draw_point_order(jax.random.fold_in(streams_of[11], 71), 0),
        "skeleton": draw_skeleton(jax.random.fold_in(streams_of[11], 71), 0),
        "root_skeleton": draw_root_skeleton(jax.random.fold_in(streams_of[11], 71), 0),
        "near_list": draw_near_list(jax.random.fold_in(streams_of[11], 71), 0),
        "far_list": draw_far_list(jax.random.fold_in(streams_of[11], 71), 0),
    }


HIGHEST_PREC = lax.Precision.HIGHEST
RIDGE_SHIFT = 1.0
EPSILON = 1e-06

def gaussian(inner_prod, target_sq, source_sq, feat_count):
    return jnp.exp(-(target_sq + source_sq - 2.0 * inner_prod) / feat_count)

def reference(points, leaf_maps, root_maps, current, krylov_basis, ritz_roots, point_order, skeleton, root_skeleton, near_list, far_list):
    feat_count = points.shape[1]
    leaf_points = points.reshape(LEAVES, LS, F)
    leaf_sq = lax.optimization_barrier(jnp.sum(leaf_points * leaf_points, axis=-1))
    skel_points = jnp.take_along_axis(leaf_points, skeleton[:, :, None], axis=1)
    skel_sq = lax.optimization_barrier(jnp.sum(skel_points * skel_points, axis=-1))
    subtree_of = (jnp.arange(LEAVES, dtype=jnp.int32) // SUBLEAVES).astype(jnp.int32)

    def to_global(window_slots):
        offset = window_slots // SUBLEAVES - 1
        return ((subtree_of[:, None] + offset) % SUBTREES * SUBLEAVES + window_slots % SUBLEAVES).astype(jnp.int32)
    near_global = to_global(near_list)
    far_global = to_global(far_list)
    far_points = skel_points[far_global]
    far_inner = jnp.einsum('bmf,bjnf->bjmn', skel_points, far_points, precision=HIGHEST_PREC)
    far_kernel = gaussian(far_inner, skel_sq[:, None, :, None], skel_sq[far_global][:, :, None, :], feat_count)
    subtree_points = points.reshape(SUBTREES, SUBLEAVES * LS, F)
    root_points = jnp.take_along_axis(subtree_points, root_skeleton[:, :, None], axis=1).reshape(SUBTREES * SK, F)
    root_sq = lax.optimization_barrier(jnp.sum(root_points * root_points, axis=-1))
    root_inner = jnp.dot(root_points, root_points.T, precision=HIGHEST_PREC)
    top_kernel = gaussian(root_inner, root_sq[:, None], root_sq[None, :], feat_count)
    distance = (jnp.arange(SUBTREES)[None, :] - jnp.arange(SUBTREES)[:, None]) % SUBTREES
    far_mask = (distance >= 1).astype(jnp.float32)
    top_kernel = top_kernel * jnp.repeat(jnp.repeat(far_mask, SK, axis=0), SK, axis=1)

    def operator(vector):
        values = vector.reshape(LEAVES, LS)
        skel_weights = jnp.einsum('bkn,bn->bk', leaf_maps, values, precision=HIGHEST_PREC)
        root_weights = jnp.einsum('bkn,bn->bk', root_maps, values, precision=HIGHEST_PREC).reshape(SUBTREES, SUBLEAVES, SK).sum(axis=1)

        def near_one(packed):
            targets, target_sq, neighbours = packed
            sources = leaf_points[neighbours]
            inner_prod = jnp.einsum('mf,jnf->jmn', targets, sources, precision=HIGHEST_PREC)
            kernel = gaussian(inner_prod, target_sq[None, :, None], leaf_sq[neighbours][:, None, :], feat_count)
            return jnp.einsum('jmn,jn->m', kernel, values[neighbours], precision=HIGHEST_PREC)
        result = lax.map(near_one, (leaf_points, leaf_sq, near_global))
        skel_out = jnp.einsum('bjmn,bjn->bm', far_kernel, skel_weights[far_global], precision=HIGHEST_PREC)
        result = result + jnp.einsum('bkn,bk->bn', leaf_maps, skel_out, precision=HIGHEST_PREC)
        root_out = jnp.dot(top_kernel, root_weights.reshape(-1), precision=HIGHEST_PREC).reshape(SUBTREES, SK)
        result = result + jnp.einsum('bkn,bk->bn', root_maps, root_out[subtree_of], precision=HIGHEST_PREC)
        return result.reshape(-1) + RIDGE_SHIFT * vector
    order_rows = point_order.reshape(SUBTREES, SUBLEAVES * LS)
    tree_vector = jnp.take_along_axis(current.reshape(SUBTREES, SUBLEAVES * LS), order_rows, axis=1).reshape(-1)
    first_section = tree_vector - operator(tree_vector) / ritz_roots[0]
    second = first_section - operator(first_section) / ritz_roots[1]
    preconditioned = (tree_vector - second).reshape(SUBTREES, SUBLEAVES * LS)
    user_grown = jax.vmap(lambda positions, entries: jnp.zeros_like(entries).at[positions].set(entries))(order_rows, preconditioned).reshape(-1)
    projections = jnp.dot(krylov_basis, user_grown, precision=HIGHEST_PREC)
    orthogonal = user_grown - jnp.dot(projections, krylov_basis, precision=HIGHEST_PREC)
    length_norm = jnp.sqrt(jnp.sum(orthogonal * orthogonal) + EPSILON)
    return (orthogonal, jnp.concatenate([projections, length_norm[None]]))
```

```python
import jax
import jax.numpy as jnp
from jax import lax
from jax.experimental import pallas as pl
from jax.experimental.pallas import tpu as pltpu
from jax.sharding import PartitionSpec as P

RIDGE_SHIFT = 1.0
EPSILON = 1e-06
LOG2E = 1.4426950408889634
LANES = 128
CHUNK = 256
UNROLL = 8
MESH = pl.DeviceIdType.MESH
VMEM = pl.BlockSpec(memory_space=pltpu.VMEM)
SMEM = pl.BlockSpec(memory_space=pltpu.SMEM)
F32, BF16 = jnp.float32, jnp.bfloat16


def bf16_part(x):
    return x.astype(BF16).astype(F32)


def augmented(x, scale, target):
    feat, size = x.shape
    sq = -scale * jnp.sum(x * x, axis=0, keepdims=True)
    s1 = bf16_part(sq)
    s2 = bf16_part(sq - s1)
    s3 = sq - s1 - s2
    row = lax.broadcasted_iota(jnp.int32, (feat, size), 0)
    first = 3 if target else 0
    ones = jnp.where(row < 6, 1.0, 0.0)
    extra = jnp.where(
        row == first,
        s1,
        jnp.where(row == first + 1, s2, jnp.where(row == first + 2, s3, ones)),
    )
    if target:
        x = x * (2.0 * scale)
    hi = bf16_part(x)
    lo = x - hi
    return (hi, lo, hi, extra) if target else (hi, hi, lo, extra)


def split3(x):
    hi = bf16_part(x)
    mid = bf16_part(x - hi)
    return hi, mid, x - hi - mid


def column_of(row):
    return jnp.broadcast_to(row, (LANES, row.shape[1])).T


def row_of(block):
    return jnp.sum(block.T, axis=0, keepdims=True)


def kernel_body(dims, *refs):
    (per, leaf_size, feat, skel, leaves, subs, near_count, far_count, basis_count) = dims
    (
        xt_ref,
        lmap_ref,
        rmap_ref,
        cur_ref,
        order_ref,
        skel_ref,
        rskel_ref,
        near_ref,
        far_ref,
        basis_ref,
        ritz_ref,
        orth_ref,
        hess_ref,
        xin_ref,
        meta_own,
        meta_in,
        cur_in,
        col_ref,
        row_ref,
        zcol_ref,
        zrow_ref,
        ntab_ref,
        ftab_ref,
        vw_ref,
        vrow_ref,
        vb_ref,
        wb_ref,
        acc1_ref,
        acc2_ref,
        fac1_ref,
        fac2_ref,
        root_own,
        root_in,
        rcol_ref,
        kroot_ref,
        wroot_own,
        wroot_in,
        rs_out,
        rs_in,
        placed_ref,
        fin_in,
        tot_own,
        tot_in,
        tot_sub,
        tot_all,
        gram_ref,
        cur_sem,
        meta_sem,
        pts_send,
        pts_recv,
        vw_sem,
        rs_sem,
        root_send,
        root_recv,
        wroot_send,
        wroot_recv,
        fin_sem,
        tots_sem,
        totl_sem,
    ) = refs
    t, s = lax.axis_index("leaf"), lax.axis_index("sub")
    chips = subs // 2
    chip, core = lax.div(s, 2), lax.rem(s, 2)
    cols = per * subs
    groups = leaf_size // LANES
    rows_own = per * leaf_size // LANES
    rows_all = subs * rows_own
    scale = LOG2E / feat
    halo = subs
    quota = -(-leaves // subs)
    next_leaf, prev_leaf = lax.rem(t + 1, leaves), lax.rem(t + leaves - 1, leaves)
    units = range(1, subs)

    def sub_of(k):
        return lax.rem(chip + k // 2, chips) * 2 + lax.rem(core + k % 2, 2)

    def sub_of_dynamic(k):
        return lax.rem(chip + lax.div(k, 2), chips) * 2 + lax.rem(core + lax.rem(k, 2), 2)

    def inverse(k):
        return (chips - k // 2) % chips * 2 + k % 2

    def upper(k):
        return lax.div(s - sub_of(k) + subs - 1, subs)

    def copy(src, dst, send, recv, there):
        return pltpu.make_async_remote_copy(
            src_ref=src, dst_ref=dst, send_sem=send, recv_sem=recv, device_id=there, device_id_type=MESH
        )

    started = []

    def start(*args):
        c = copy(*args)
        c.start()
        started.append(c)

    def arrived(dst, send, recv):
        copy(dst, dst, send, recv, (t, sub_of(1))).wait_recv()

    barrier = pltpu.get_barrier_semaphore()
    peers = [(t, sub_of(k)) for k in units]
    peers += [(lax.rem(t + d, leaves), s) for d in range(1, leaves)]
    for there in peers:
        pl.semaphore_signal(barrier, inc=1, device_id=there, device_id_type=MESH)

    meta_own[...] = jnp.zeros_like(meta_own)
    meta_own[:, 0:skel] = skel_ref[...].astype(F32)
    meta_own[:, LANES : LANES + near_count] = near_ref[...].astype(F32)
    meta_own[:, 2 * LANES : 2 * LANES + far_count] = far_ref[...].astype(F32)
    pl.semaphore_wait(barrier, len(peers))
    for k in units:
        start(cur_ref, cur_in.at[inverse(k) - 1], cur_sem.at[0, k - 1], cur_sem.at[1, inverse(k) - 1], (t, sub_of(k)))
    across = [k for k in units if k % 2 == 0]
    sibling = 1
    for j in range(per):
        for k in across:
            start(
                xt_ref.at[j],
                xin_ref.at[inverse(k), j],
                pts_send.at[k, j],
                pts_recv.at[inverse(k), j],
                (t, sub_of(k)),
            )
        start(xt_ref.at[j], xin_ref.at[halo, j], pts_send.at[halo, j], pts_recv.at[halo, j], (prev_leaf, s))
        start(
            xt_ref.at[j],
            xin_ref.at[sibling, j],
            pts_send.at[sibling, j],
            pts_recv.at[sibling, j],
            (t, sub_of(sibling)),
        )
    for k in units:
        start(
            meta_own,
            meta_in.at[inverse(k) - 1],
            meta_sem.at[0, k - 1],
            meta_sem.at[1, inverse(k) - 1],
            (t, sub_of(k)),
        )
    start(meta_own, meta_in.at[halo - 1], meta_sem.at[0, halo - 1], meta_sem.at[1, halo - 1], (prev_leaf, s))

    def build_col(c, x):
        for i, piece in enumerate(augmented(x, scale, False)):
            col_ref[c, i * feat : (i + 1) * feat] = piece.astype(BF16)

    def build_row(r, x):
        pieces = augmented(x, scale, True)
        row_ref[r] = jnp.concatenate(pieces, axis=0).T.astype(BF16)

    def one_hot(index_row):
        spot = lax.broadcasted_iota(jnp.int32, (leaf_size, skel), 0)
        return jnp.where(spot == index_row, 1.0, 0.0)

    def meta_row(k, j, lane, count):
        if k == 0:
            return meta_own[j : j + 1, lane : lane + count]
        return meta_in[k - 1, j : j + 1, lane : lane + count]

    def build_tables(k, j):
        place = k * per + j
        slots = lax.broadcasted_iota(jnp.int32, (3 * cols, 1), 0).astype(F32)
        for table, lane, count in ((ntab_ref, LANES, near_count), (ftab_ref, 2 * LANES, far_count)):
            hit = jnp.where(slots == meta_row(k, j, lane, count), 1.0, 0.0)
            table[place] = jnp.broadcast_to(jnp.max(hit, axis=1, keepdims=True), (3 * cols, LANES))

    def build_skeleton(k, j, as_col, r):
        chosen = one_hot(meta_row(k, j, 0, skel).astype(jnp.int32))
        if as_col:
            picked = jnp.dot(col_ref[k * per + j], chosen.astype(BF16), preferred_element_type=F32)
            zcol_ref[k, :, j * skel : (j + 1) * skel] = picked.astype(BF16)
        if r is not None:
            picked = jnp.dot(chosen.T.astype(BF16), row_ref[r], preferred_element_type=F32)
            zrow_ref[r // per, j * skel : (j + 1) * skel, :] = picked.astype(BF16)

    for j in range(per):
        build_col(j, xt_ref[j])
        build_row(j, xt_ref[j])
    for j in range(per):
        build_tables(0, j)
        build_skeleton(0, j, True, j)
    gram = jnp.zeros((basis_count, LANES), F32)
    lane_small = lax.broadcasted_iota(jnp.int32, (basis_count, LANES), 1)
    sub_small = lax.broadcasted_iota(jnp.int32, (basis_count, LANES), 0)
    for i in range(basis_count):
        total = jnp.zeros((basis_count, LANES), F32)
        for r in range(rows_own):
            piece = basis_ref[:, r * LANES : (r + 1) * LANES]
            total = total + piece * piece[i : i + 1]
        gram = gram + jnp.where(lane_small == 1 + i, jnp.sum(total, axis=1, keepdims=True), 0.0)
    gram_ref[...] = gram

    for k in units:
        arrived(cur_in.at[k - 1], cur_sem.at[0, k - 1], cur_sem.at[1, k - 1])
    row_spot = lax.broadcasted_iota(jnp.int32, (rows_all, leaf_size), 0)
    lane_spot = lax.broadcasted_iota(jnp.int32, (LANES, leaf_size), 0)
    depth = -(-3 * rows_all // LANES) * LANES
    placed_ref[s] = cur_ref[...]
    for k in units:
        placed_ref[sub_of(k)] = cur_in[k - 1]
    pieces = split3(placed_ref[...].reshape(rows_all, LANES))
    pad = [jnp.zeros((depth - 3 * rows_all, LANES), F32)] if depth > 3 * rows_all else []
    stack = jnp.concatenate(list(pieces) + pad, axis=0).T.astype(BF16)

    def hot_rows(j):
        index = order_ref[j : j + 1, :]
        return (
            row_spot == lax.shift_right_logical(index, 7),
            lane_spot == lax.bitwise_and(index, LANES - 1),
        )

    tree = []
    for j in range(per):
        in_row, in_lane = hot_rows(j)
        hot = jnp.where(in_row, 1.0, 0.0)
        fill = [jnp.zeros((depth - 3 * rows_all, leaf_size), F32)] if depth > 3 * rows_all else []
        picked = jnp.dot(
            stack, jnp.concatenate([hot] * 3 + fill, axis=0).astype(BF16), preferred_element_type=F32
        )
        tree.append(jnp.sum(jnp.where(in_lane, picked, 0.0), axis=0, keepdims=True))

    def weigh(p, vectors):
        total = jnp.zeros((skel, LANES), F32)
        for j in range(per):
            part = jnp.zeros((skel, LANES), F32)
            for g in range(groups):
                piece = vectors[j][:, g * LANES : (g + 1) * LANES]
                part = part + lmap_ref[j, :, g * LANES : (g + 1) * LANES] * piece
                total = total + rmap_ref[j, :, g * LANES : (g + 1) * LANES] * piece
            vw_ref[p, 0, j : j + 1, 0:leaf_size] = vectors[j]
            vw_ref[p, 0, j : j + 1, leaf_size : leaf_size + skel] = row_of(part)
        vw_ref[p, 0, per : per + 1, 0:skel] = row_of(total)
        for k in units:
            start(
                vw_ref.at[p, 0],
                vw_ref.at[p, inverse(k)],
                vw_sem.at[p, 0, k - 1],
                vw_sem.at[p, 1, inverse(k) - 1],
                (t, sub_of(k)),
            )
        start(
            vw_ref.at[p, 0],
            vw_ref.at[p, halo],
            vw_sem.at[p, 0, halo - 1],
            vw_sem.at[p, 1, halo - 1],
            (prev_leaf, s),
        )

    def near_block(r, c, m1, m2):
        va = None
        if m2 is not None:
            va = [
                jnp.broadcast_to(vrow_ref[c, :, g * LANES : (g + 1) * LANES] * m2, (8, LANES))
                for g in range(groups)
            ]
        acc = [jnp.zeros((8, LANES), F32) for _ in range(groups)]
        for m in range(0, leaf_size, CHUNK):
            inner = jnp.dot(row_ref[r, m : m + CHUNK], col_ref[c], preferred_element_type=F32)
            for h in range(0, CHUNK, 8):
                e = jnp.exp2(inner[h : h + 8])
                w = vb_ref[r, m + h : m + h + 8]
                tot = None
                for g in range(groups):
                    piece = e[:, g * LANES : (g + 1) * LANES]
                    acc[g] = acc[g] + piece * w
                    if va is not None:
                        q = piece * va[g]
                        tot = q if tot is None else tot + q
                if va is not None:
                    acc2_ref[r, m + h : m + h + 8] += tot
        for g in range(groups):
            acc1_ref[c, :, g * LANES : (g + 1) * LANES] += acc[g] * m1

    def table_row(table, place, slot):
        return table[place, pl.ds(slot, 1), :]

    def own_pair(r, c, k, j, both=True):
        m1 = table_row(ntab_ref, c, cols + s * per + r)
        m2 = table_row(ntab_ref, r, cols + sub_of(k) * per + j) if both else None
        near_block(r, c, m1, m2)

    def near_self():
        def diagonal(i, carry):
            own_pair(i, i, 0, i, False)
            return carry

        lax.fori_loop(0, per, diagonal, 0, unroll=per)
        for d in range(1, per // 2 + 1):
            count = per if 2 * d < per else per // 2

            def pair(i, carry):
                j = lax.rem(i + d, per)
                own_pair(i, j, 0, j)
                return carry

            lax.fori_loop(0, count, pair, 0, unroll=count)

    def near_unit(k):
        half = per // 2

        def pair(b, carry):
            o = lax.div(b, half)
            j = 2 * lax.rem(b, half) + lax.rem(o + upper(k), 2)
            own_pair(o, k * per + j, k, j)
            return carry

        lax.fori_loop(0, per * half, pair, 0, unroll=per * half)

    def near_halo():
        def outer(i, carry):
            def pair(c, carry):
                place = sub_of_dynamic(lax.div(c, per)) * per + lax.rem(c, per)
                m1 = table_row(ntab_ref, c, 2 * cols + s * per + i)
                m2 = table_row(ntab_ref, cols + i, place)
                near_block(per + i, c, m1, m2)
                return carry

            return lax.fori_loop(0, cols, pair, carry, unroll=UNROLL)

        lax.fori_loop(0, per, outer, 0)

    def far_block(p, r, k, parity):
        inner = jnp.dot(zrow_ref[r], zcol_ref[k], preferred_element_type=F32)
        both = parity is not None or r == 1
        for i in range(per):
            acc = [jnp.zeros((8, LANES), F32) for _ in range(per)]
            ways = []
            for j in range(per):
                peer = (sub_of(k) if r == 0 else sub_of_dynamic(k)) * per + j
                slot = (cols if r == 0 else 2 * cols) + s * per + i
                m1 = table_row(ftab_ref, k * per + j, slot)
                m2 = table_row(ftab_ref, i if r == 0 else cols + i, (cols if r == 0 else 0) + peer)
                if parity is not None:
                    use = (1 - lax.rem(parity + i + j, 2)).astype(F32)
                    m1, m2 = m1 * use, m2 * use
                w = vw_ref[p, k, j : j + 1, leaf_size : leaf_size + skel]
                ways.append((m1, jnp.broadcast_to(w * m2, (8, LANES))))
            for h in range(i * skel, (i + 1) * skel, 8):
                e = jnp.exp2(inner[h : h + 8])
                wb = wb_ref[r, h : h + 8]
                tot = None
                for j in range(per):
                    piece = e[:, j * skel : (j + 1) * skel]
                    acc[j] = acc[j] + piece * wb
                    if both:
                        q = piece * ways[j][1]
                        tot = q if tot is None else tot + q
                if both:
                    fac2_ref[r, h : h + 8] += tot
            for j in range(per):
                fac1_ref[k, :, j * skel : (j + 1) * skel] += acc[j] * ways[j][0]

    def spread(p, k):
        for j in range(per):
            value = vw_ref[p, k, j : j + 1, 0:leaf_size]
            if k != halo:
                vrow_ref[k * per + j] = value
            if k in (0, halo):
                r = j if k == 0 else per + j
                vb_ref[r] = column_of(value)
                wb_ref[r // per, j * skel : (j + 1) * skel] = column_of(
                    vw_ref[p, k, j : j + 1, leaf_size : leaf_size + skel]
                )

    def wait_vw(p, k):
        arrived(vw_ref.at[p, k], vw_sem.at[p, 0, k - 1], vw_sem.at[p, 1, k - 1])

    def clear():
        acc1_ref[...] = jnp.zeros_like(acc1_ref)
        acc2_ref[...] = jnp.zeros_like(acc2_ref)
        fac1_ref[...] = jnp.zeros_like(fac1_ref)
        fac2_ref[...] = jnp.zeros_like(fac2_ref)

    home = lax.rem(t, subs)

    def send_root_weights(p):
        total = vw_ref[p, 0, per : per + 1, 0:skel]
        for k in units:
            total = total + vw_ref[p, k, per : per + 1, 0:skel]
        wroot_own[p] = jnp.broadcast_to(total, (8, skel))

        @pl.when(s == home)
        def _():
            for d in range(1, leaves):
                copy(
                    wroot_own.at[p],
                    wroot_in.at[p, lax.div(t, subs)],
                    wroot_send.at[p, d - 1],
                    wroot_recv.at[p, lax.div(t, subs)],
                    (lax.rem(t + d, leaves), s),
                ).start()

    def root_of(q):
        return q * subs + s

    def present(q):
        u = root_of(q)
        return jnp.logical_and(u != t, u < leaves)

    def top(p):
        total = jnp.zeros((8, LANES), F32)
        for q in range(quota):

            @pl.when(present(q))
            def _():
                arrived(wroot_in.at[p, q], wroot_send.at[p, 0], wroot_recv.at[p, q])

            @pl.when(jnp.logical_not(present(q)))
            def _():
                wroot_in[p, q] = jnp.zeros((8, skel), F32)

            column = column_of(wroot_in[p, q, 0:1, :])
            for h in range(0, skel, 8):
                total = total + kroot_ref[q, h : h + 8] * column[h : h + 8]
        return jnp.sum(total, axis=0, keepdims=True)

    def reduce_start(p):
        root_out = top(p)
        for k in units:
            for j in range(per):
                c = k * per + j
                rs_out[p, k, j : j + 1, 0:leaf_size] = jnp.sum(acc1_ref[c], axis=0, keepdims=True)
            rs_out[p, k, 0:per, leaf_size : leaf_size + skel] = jnp.concatenate(
                [
                    jnp.sum(fac1_ref[k, :, j * skel : (j + 1) * skel], axis=0, keepdims=True)
                    for j in range(per)
                ],
                axis=0,
            )
            rs_out[p, k, per : per + 1, 0:skel] = root_out
            start(
                rs_out.at[p, k],
                rs_in.at[p, inverse(k) - 1],
                rs_sem.at[p, 0, k - 1],
                rs_sem.at[p, 1, inverse(k) - 1],
                (t, sub_of(k)),
            )
        for j in range(per):
            rs_out[p, 0, j : j + 1, 0:leaf_size] = row_of(acc2_ref[per + j])
            rs_out[p, 0, j : j + 1, leaf_size : leaf_size + skel] = row_of(
                fac2_ref[1, j * skel : (j + 1) * skel]
            )
        start(
            rs_out.at[p, 0],
            rs_in.at[p, halo - 1],
            rs_sem.at[p, 0, halo - 1],
            rs_sem.at[p, 1, halo - 1],
            (next_leaf, s),
        )
        return root_out

    def reduce_finish(p, root_out):
        nears, fars = [], []
        for j in range(per):
            nears.append(jnp.sum(acc1_ref[j], axis=0, keepdims=True) + row_of(acc2_ref[j]))
            fars.append(
                jnp.sum(fac1_ref[0, :, j * skel : (j + 1) * skel], axis=0, keepdims=True)
                + row_of(fac2_ref[0, j * skel : (j + 1) * skel])
            )
        for k in range(1, subs + 1):
            arrived(rs_in.at[p, k - 1], rs_sem.at[p, 0, k - 1], rs_sem.at[p, 1, k - 1])
            for j in range(per):
                nears[j] = nears[j] + rs_in[p, k - 1, j : j + 1, 0:leaf_size]
                fars[j] = fars[j] + rs_in[p, k - 1, j : j + 1, leaf_size : leaf_size + skel]
            if k < subs:
                root_out = root_out + rs_in[p, k - 1, per : per + 1, 0:skel]
        root_column = column_of(root_out)
        applied = []
        for j in range(per):
            far_column = column_of(fars[j])
            parts = []
            for g in range(groups):
                lanes = slice(g * LANES, (g + 1) * LANES)
                both = lmap_ref[j, :, lanes] * far_column + rmap_ref[j, :, lanes] * root_column
                parts.append(jnp.sum(both, axis=0, keepdims=True))
            applied.append(nears[j] + jnp.concatenate(parts, axis=1))
        return applied

    weigh(0, tree)
    spread(0, 0)
    clear()
    near_self()
    far_block(0, 0, 0, None)

    def take_points(k, forward):
        for j in range(per):
            arrived(xin_ref.at[k, j], pts_send.at[k, j], pts_recv.at[k, j])
            if forward:
                start(
                    xin_ref.at[k, j],
                    xin_ref.at[k + 1, j],
                    pts_send.at[k + 1, j],
                    pts_recv.at[k + 1, j],
                    (t, sub_of(sibling)),
                )
        for j in range(per):
            build_col(k * per + j, xin_ref[k, j])
            build_tables(k, j)
            build_skeleton(k, j, True, None)

    for k in units:
        arrived(meta_in.at[k - 1], meta_sem.at[0, k - 1], meta_sem.at[1, k - 1])
        wait_vw(0, k)
        spread(0, k)
    arrived(meta_in.at[halo - 1], meta_sem.at[0, halo - 1], meta_sem.at[1, halo - 1])
    send_root_weights(0)
    for k in [sibling] + across + [k for k in units if k % 2 == 1 and k != sibling]:
        take_points(k, k in across)
        near_unit(k)
        far_block(0, 0, k, upper(k))

    root_points = jnp.zeros((4 * feat, skel), F32)
    for k in range(subs):
        for j in range(per):
            base = (sub_of(k) * per + j) * leaf_size
            chosen = one_hot(rskel_ref[...] - base)
            root_points = root_points + jnp.dot(
                col_ref[k * per + j], chosen.astype(BF16), preferred_element_type=F32
            )
    rcol_ref[...] = root_points.astype(BF16)
    root_own[...] = root_points[0:feat] + root_points[2 * feat : 3 * feat]

    @pl.when(s == home)
    def _():
        for d in range(1, leaves):
            copy(
                root_own,
                root_in.at[lax.div(t, subs)],
                root_send.at[d - 1],
                root_recv.at[lax.div(t, subs)],
                (lax.rem(t + d, leaves), s),
            ).start()

    for j in range(per):
        arrived(xin_ref.at[halo, j], pts_send.at[halo, j], pts_recv.at[halo, j])
        build_row(per + j, xin_ref[halo, j])
        build_tables(halo, j)
        build_skeleton(halo, j, False, per + j)
    wait_vw(0, halo)
    spread(0, halo)
    near_halo()

    def far_halo(p):
        def step(k, carry):
            far_block(p, 1, k, None)
            return carry

        lax.fori_loop(0, subs, step, 0)

    far_halo(0)
    for q in range(quota):

        @pl.when(present(q))
        def _():
            arrived(root_in.at[q], root_send.at[0], root_recv.at[q])

        @pl.when(jnp.logical_not(present(q)))
        def _():
            root_in[q] = root_own[...]

        rows = jnp.concatenate(augmented(root_in[q], scale, True), axis=0).T.astype(BF16)
        kroot_ref[q] = jnp.exp2(jnp.dot(rows, rcol_ref[...], preferred_element_type=F32))

    root_out = reduce_start(0)
    applied = reduce_finish(0, root_out)
    first = [tree[j] - (applied[j] + RIDGE_SHIFT * tree[j]) / ritz_ref[0] for j in range(per)]

    weigh(1, first)
    spread(1, 0)
    clear()
    near_self()
    far_block(1, 0, 0, None)
    for k in units:
        wait_vw(1, k)
        spread(1, k)
    send_root_weights(1)
    for k in units:
        near_unit(k)
        far_block(1, 0, k, upper(k))
    wait_vw(1, halo)
    spread(1, halo)
    near_halo()
    far_halo(1)
    root_out = reduce_start(1)
    applied = reduce_finish(1, root_out)
    placed = jnp.zeros((rows_all, LANES), F32)
    for j in range(per):
        v0 = vw_ref[0, 0, j : j + 1, 0:leaf_size]
        v1 = vw_ref[1, 0, j : j + 1, 0:leaf_size]
        second = v1 - (applied[j] + RIDGE_SHIFT * v1) / ritz_ref[1]
        in_row, in_lane = hot_rows(j)
        held = jnp.concatenate(split3(jnp.where(in_row, v0 - second, 0.0)), axis=0)
        hot = jnp.where(in_lane, 1.0, 0.0).astype(BF16)
        spots = lax.dot_general(
            held.astype(BF16), hot, (((1,), (1,)), ((), ())), preferred_element_type=F32
        )
        placed = placed + (
            spots[0:rows_all] + spots[rows_all : 2 * rows_all] + spots[2 * rows_all : 3 * rows_all]
        )
    placed_ref[...] = placed.reshape(subs, rows_own, LANES)
    for k in units:
        start(
            placed_ref.at[sub_of(k)],
            fin_in.at[inverse(k) - 1],
            fin_sem.at[0, k - 1],
            fin_sem.at[1, inverse(k) - 1],
            (t, sub_of(k)),
        )
    user = placed_ref[s]
    for k in units:
        arrived(fin_in.at[k - 1], fin_sem.at[0, k - 1], fin_sem.at[1, k - 1])
        user = user + fin_in[k - 1]

    part = jnp.zeros((basis_count, LANES), F32)
    for r in range(rows_own):
        part = part + basis_ref[:, r * LANES : (r + 1) * LANES] * user[r : r + 1]
    square = jnp.sum(jnp.sum(user * user, axis=0, keepdims=True), axis=1, keepdims=True)
    corner = jnp.logical_and(lane_small == 1 + basis_count, sub_small == 0)
    tot_own[...] = (
        gram_ref[...]
        + jnp.where(lane_small == 0, jnp.sum(part, axis=1, keepdims=True), 0.0)
        + jnp.where(corner, square, 0.0)
    )
    for k in units:
        start(
            tot_own,
            tot_in.at[inverse(k) - 1],
            tots_sem.at[0, k - 1],
            tots_sem.at[1, inverse(k) - 1],
            (t, sub_of(k)),
        )
    total = tot_own[...]
    for k in units:
        arrived(tot_in.at[k - 1], tots_sem.at[0, k - 1], tots_sem.at[1, k - 1])
    tot_all[0] = tot_own[...]
    for k in units:
        tot_all[k] = tot_in[k - 1]
    total = tot_all[sub_order(chip, core, 0, chips)]
    for i in range(1, subs):
        total = total + tot_all[sub_order(chip, core, i, chips)]
    tot_sub[t] = total
    for d in range(1, leaves):
        start(
            tot_sub.at[t],
            tot_sub.at[t],
            totl_sem.at[0, d - 1],
            totl_sem.at[1, d - 1],
            (lax.rem(t + d, leaves), s),
        )
    for d in range(1, leaves):
        slot = tot_sub.at[lax.rem(t + leaves - d, leaves)]
        arrived(slot, totl_sem.at[0, d - 1], totl_sem.at[1, d - 1])
    total = tot_sub[0]
    for u in range(1, leaves):
        total = total + tot_sub[u]
    proj = total[:, 0:1]
    squares = jnp.sum(jnp.where(corner, total, 0.0), keepdims=True)
    proj_row = jnp.sum(jnp.where(lane_small == 1 + sub_small, proj, 0.0), axis=0, keepdims=True)
    gram_proj = jnp.sum(
        jnp.where(jnp.logical_and(lane_small >= 1, lane_small <= basis_count), total, 0.0) * proj_row,
        axis=1,
        keepdims=True,
    )
    length_sq = (
        squares
        - 2.0 * jnp.sum(proj * proj, axis=0, keepdims=True)
        + jnp.sum(proj * gram_proj, axis=0, keepdims=True)
    )
    norm = jnp.sqrt(length_sq + EPSILON)
    hess = jnp.sum(jnp.where(lane_small == sub_small, proj, 0.0), axis=0, keepdims=True)
    hess_ref[...] = hess + jnp.where(lane_small[0:1] == basis_count, norm, 0.0)
    for r in range(rows_own):
        span = jnp.sum(basis_ref[:, r * LANES : (r + 1) * LANES] * proj, axis=0, keepdims=True)
        orth_ref[r : r + 1] = user[r : r + 1] - span

    for c in started:
        c.wait_send()

    @pl.when(s == home)
    def _():
        there = (next_leaf, s)
        for d in range(1, leaves):
            q = lax.div(t, subs)
            copy(root_own, root_in.at[q], root_send.at[d - 1], root_recv.at[q], there).wait_send()
            for p in range(2):
                copy(
                    wroot_own.at[p], wroot_in.at[p, q], wroot_send.at[p, d - 1], wroot_recv.at[p, q], there
                ).wait_send()


def sub_order(chip, core, i, chips):
    return lax.rem(i // 2 + chips - chip, chips) * 2 + lax.rem(i % 2 + 2 - core, 2)


def shards(
    points,
    leaf_maps,
    root_maps,
    current,
    krylov_basis,
    ritz_roots,
    point_order,
    skeleton,
    root_skeleton,
    near_list,
    far_list,
):
    per, skel, leaf_size = leaf_maps.shape
    feat = points.shape[1]
    subs, leaves = lax.axis_size("sub"), lax.axis_size("leaf")
    near_count, far_count = near_list.shape[1], far_list.shape[1]
    basis_count = krylov_basis.shape[0]
    dims = (per, leaf_size, feat, skel, leaves, subs, near_count, far_count, basis_count)
    cols, rows_own = per * subs, per * leaf_size // LANES
    quota = -(-leaves // subs)
    xt = points.reshape(per, leaf_size, feat).transpose(0, 2, 1)
    wide = leaf_size + skel
    dma = pltpu.SemaphoreType.DMA
    scratch = [
        pltpu.VMEM((subs + 1, per, feat, leaf_size), F32),
        pltpu.VMEM((per, leaf_size), F32),
        pltpu.VMEM((subs, per, leaf_size), F32),
        pltpu.VMEM((subs - 1, rows_own, LANES), F32),
        pltpu.VMEM((cols, 4 * feat, leaf_size), BF16),
        pltpu.VMEM((2 * per, leaf_size, 4 * feat), BF16),
        pltpu.VMEM((subs, 4 * feat, per * skel), BF16),
        pltpu.VMEM((2, per * skel, 4 * feat), BF16),
        pltpu.VMEM((cols + per, 3 * cols, LANES), F32),
        pltpu.VMEM((cols + per, 3 * cols, LANES), F32),
        pltpu.VMEM((2, subs + 1, 2 * per, wide), F32),
        pltpu.VMEM((cols, 1, leaf_size), F32),
        pltpu.VMEM((2 * per, leaf_size, LANES), F32),
        pltpu.VMEM((2, per * skel, LANES), F32),
        pltpu.VMEM((cols, 8, leaf_size), F32),
        pltpu.VMEM((2 * per, leaf_size, LANES), F32),
        pltpu.VMEM((subs, 8, per * skel), F32),
        pltpu.VMEM((2, per * skel, LANES), F32),
        pltpu.VMEM((feat, skel), F32),
        pltpu.VMEM((quota, feat, skel), F32),
        pltpu.VMEM((4 * feat, skel), BF16),
        pltpu.VMEM((quota, skel, LANES), F32),
        pltpu.VMEM((2, 8, skel), F32),
        pltpu.VMEM((2, quota, 8, skel), F32),
        pltpu.VMEM((2, subs, 2 * per, wide), F32),
        pltpu.VMEM((2, subs, 2 * per, wide), F32),
        pltpu.VMEM((subs, rows_own, LANES), F32),
        pltpu.VMEM((subs - 1, rows_own, LANES), F32),
        pltpu.VMEM((basis_count, LANES), F32),
        pltpu.VMEM((subs - 1, basis_count, LANES), F32),
        pltpu.VMEM((leaves, basis_count, LANES), F32),
        pltpu.VMEM((subs, basis_count, LANES), F32),
        pltpu.VMEM((basis_count, LANES), F32),
        dma((2, subs - 1)),
        dma((2, subs)),
        dma((subs + 1, per)),
        dma((subs + 1, per)),
        dma((2, 2, subs)),
        dma((2, 2, subs)),
        dma((leaves - 1,)),
        dma((quota,)),
        dma((2, leaves - 1)),
        dma((2, quota)),
        dma((2, subs - 1)),
        dma((2, subs - 1)),
        dma((2, leaves - 1)),
    ]
    orth, hess = pl.pallas_call(
        lambda *refs: kernel_body(dims, *refs),
        out_shape=[
            jax.ShapeDtypeStruct((rows_own, LANES), F32),
            jax.ShapeDtypeStruct((1, LANES), F32),
        ],
        in_specs=[VMEM] * 10 + [SMEM],
        out_specs=[VMEM] * 2,
        scratch_shapes=scratch,
        compiler_params=pltpu.CompilerParams(
            collective_id=0, has_side_effects=True, vmem_limit_bytes=48 * 1024 * 1024
        ),
        name="step",
    )(
        xt,
        leaf_maps,
        root_maps,
        current.reshape(rows_own, LANES),
        point_order.reshape(per, leaf_size),
        skeleton,
        root_skeleton,
        near_list,
        far_list,
        krylov_basis,
        ritz_roots,
    )
    return orth.reshape(-1), hess[0, : basis_count + 1]


def solution(mesh):
    return jax.shard_map(
        shards,
        mesh=mesh,
        in_specs=(
            P(("leaf", "sub"), None),
            P(("leaf", "sub"), None, None),
            P(("leaf", "sub"), None, None),
            P(("leaf", "sub")),
            P(None, ("leaf", "sub")),
            P(),
            P(("leaf", "sub")),
            P(("leaf", "sub"), None),
            P("leaf", None),
            P(("leaf", "sub"), None),
            P(("leaf", "sub"), None),
        ),
        out_specs=(P(("leaf", "sub")), P()),
        check_vma=False,
    )
```

```python
import jax
import jax.numpy as jnp
from jax import lax
from jax.experimental import pallas as pl
from jax.experimental.pallas import tpu as pltpu
from jax.sharding import PartitionSpec as P

RIDGE_SHIFT = 1.0
EPSILON = 1e-06
LOG2E = 1.4426950408889634
LANES = 128
CHUNK = 256
MESH = pl.DeviceIdType.MESH
VMEM = pl.BlockSpec(memory_space=pltpu.VMEM)
SMEM = pl.BlockSpec(memory_space=pltpu.SMEM)
F32, BF16 = jnp.float32, jnp.bfloat16


def bf16_part(x):
    return x.astype(BF16).astype(F32)


def augmented(x, scale, target):
    feat, size = x.shape
    sq = -scale * jnp.sum(x * x, axis=0, keepdims=True)
    s1 = bf16_part(sq)
    s2 = bf16_part(sq - s1)
    s3 = sq - s1 - s2
    row = lax.broadcasted_iota(jnp.int32, (feat, size), 0)
    first = 3 if target else 0
    ones = jnp.where(row < 6, 1.0, 0.0)
    extra = jnp.where(
        row == first,
        s1,
        jnp.where(row == first + 1, s2, jnp.where(row == first + 2, s3, ones)),
    )
    if target:
        x = x * (2.0 * scale)
    hi = bf16_part(x)
    lo = x - hi
    return (hi, lo, hi, extra) if target else (hi, hi, lo, extra)


def split3(x):
    hi = bf16_part(x)
    mid = bf16_part(x - hi)
    return hi, mid, x - hi - mid


def column_of(row):
    return jnp.broadcast_to(row, (LANES, row.shape[1])).T


def fold(block):
    return jnp.sum(block.reshape(block.shape[0] // 8, 8, LANES), axis=0)


def row_of(block):
    return jnp.sum(block.T, axis=0, keepdims=True)


def kernel_body(dims, *refs):
    (per, leaf_size, feat, skel, leaves, subs, near_count, far_count, basis_count) = dims
    (
        xt_ref,
        lmap_ref,
        rmap_ref,
        cur_ref,
        order_ref,
        skel_ref,
        rskel_ref,
        near_ref,
        far_ref,
        basis_ref,
        ritz_ref,
        orth_ref,
        hess_ref,
        xin_ref,
        meta_own,
        meta_in,
        cur_in,
        ord_in,
        bas_in,
        col_ref,
        row_ref,
        zcol_ref,
        zrow_ref,
        ntab_ref,
        ftab_ref,
        vw_ref,
        vrow_ref,
        vb_ref,
        wb_ref,
        acc1_ref,
        acc2_ref,
        fac1_ref,
        fac2_ref,
        root_own,
        root_in,
        rcol_ref,
        kroot_ref,
        wroot_own,
        wroot_in,
        rs_out,
        rs_in,
        placed_ref,
        fin_in,
        tot_own,
        tot_in,
        tot_sub,
        tot_all,
        gram_ref,
        cur_sem,
        ord_sem,
        bas_sem,
        meta_sem,
        pts_send,
        pts_recv,
        vw_sem,
        rs_sem,
        root_send,
        root_recv,
        wroot_send,
        wroot_recv,
        fin_sem,
        tots_sem,
        totl_sem,
    ) = refs
    t, s = lax.axis_index("leaf"), lax.axis_index("sub")
    chips = subs // 2
    chip, core = lax.div(s, 2), lax.rem(s, 2)
    cols = per * subs
    groups = leaf_size // LANES
    rows_own = per * leaf_size // LANES
    rows_all = subs * rows_own
    scale = LOG2E / feat
    halo = subs
    quota = -(-leaves // subs)
    next_leaf, prev_leaf = lax.rem(t + 1, leaves), lax.rem(t + leaves - 1, leaves)
    units = range(1, subs)

    def sub_of(k):
        return lax.rem(chip + k // 2, chips) * 2 + lax.rem(core + k % 2, 2)

    def sub_of_dynamic(k):
        return lax.rem(chip + lax.div(k, 2), chips) * 2 + lax.rem(core + lax.rem(k, 2), 2)

    def inverse(k):
        return (chips - k // 2) % chips * 2 + k % 2

    def upper(k):
        return lax.div(s - sub_of(k) + subs - 1, subs)

    def copy(src, dst, send, recv, there):
        return pltpu.make_async_remote_copy(
            src_ref=src, dst_ref=dst, send_sem=send, recv_sem=recv, device_id=there, device_id_type=MESH
        )

    started = []

    def start(*args):
        c = copy(*args)
        c.start()
        started.append(c)

    def arrived(dst, send, recv):
        copy(dst, dst, send, recv, (t, sub_of(1))).wait_recv()

    barrier = pltpu.get_barrier_semaphore()
    peers = [(t, sub_of(k)) for k in units]
    peers += [(lax.rem(t + d, leaves), s) for d in range(1, leaves)]
    for there in peers:
        pl.semaphore_signal(barrier, inc=1, device_id=there, device_id_type=MESH)

    meta_own[...] = jnp.zeros_like(meta_own)
    meta_own[:, 0:skel] = skel_ref[...].astype(F32)
    meta_own[:, LANES : LANES + near_count] = near_ref[...].astype(F32)
    meta_own[:, 2 * LANES : 2 * LANES + far_count] = far_ref[...].astype(F32)
    pl.semaphore_wait(barrier, len(peers))
    def send_units(src, dst, sem):
        for k in units:
            start(src, dst.at[inverse(k) - 1], sem.at[0, k - 1], sem.at[1, inverse(k) - 1], (t, sub_of(k)))

    across = [k for k in units if k % 2 == 0]
    sibling = 1

    def send_points(j):
        to = [(k, inverse(k), (t, sub_of(k))) for k in across]
        to += [(halo, halo, (prev_leaf, s)), (sibling, sibling, (t, sub_of(sibling)))]
        for k, slot, there in to:
            start(xt_ref.at[j], xin_ref.at[slot, j], pts_send.at[k, j], pts_recv.at[slot, j], there)

    early = per // 2
    send_units(cur_ref, cur_in, cur_sem)
    send_units(order_ref, ord_in, ord_sem)
    send_units(meta_own, meta_in, meta_sem)
    start(meta_own, meta_in.at[halo - 1], meta_sem.at[0, halo - 1], meta_sem.at[1, halo - 1], (prev_leaf, s))
    for j in range(early):
        send_points(j)

    def build_col(c, x):
        for i, piece in enumerate(augmented(x, scale, False)):
            col_ref[c, i * feat : (i + 1) * feat] = piece.astype(BF16)

    def build_row(r, x):
        pieces = augmented(x, scale, True)
        row_ref[r] = jnp.concatenate(pieces, axis=0).T.astype(BF16)

    def one_hot(index_row):
        spot = lax.broadcasted_iota(jnp.int32, (leaf_size, skel), 0)
        return jnp.where(spot == index_row, 1.0, 0.0)

    def meta_row(k, j, lane, count):
        if k == 0:
            return meta_own[j : j + 1, lane : lane + count]
        return meta_in[k - 1, j : j + 1, lane : lane + count]

    def build_tables(k, j):
        place = k * per + j
        slots = lax.broadcasted_iota(jnp.int32, (3 * cols, 1), 0).astype(F32)
        for table, lane, count in ((ntab_ref, LANES, near_count), (ftab_ref, 2 * LANES, far_count)):
            hit = jnp.where(slots == meta_row(k, j, lane, count), 1.0, 0.0)
            table[place] = jnp.broadcast_to(jnp.max(hit, axis=1, keepdims=True), (3 * cols, LANES))

    def build_skeleton(k, j, as_col, r):
        chosen = one_hot(meta_row(k, j, 0, skel).astype(jnp.int32))
        if as_col:
            picked = jnp.dot(col_ref[k * per + j], chosen.astype(BF16), preferred_element_type=F32)
            zcol_ref[k, :, j * skel : (j + 1) * skel] = picked.astype(BF16)
        if r is not None:
            picked = jnp.dot(chosen.T.astype(BF16), row_ref[r], preferred_element_type=F32)
            zrow_ref[r // per, j * skel : (j + 1) * skel, :] = picked.astype(BF16)

    for j in range(per):
        build_col(j, xt_ref[j])
        build_row(j, xt_ref[j])
    for j in range(per):
        build_tables(0, j)
        build_skeleton(0, j, True, j)
    gram = jnp.zeros((basis_count, LANES), F32)
    lane_small = lax.broadcasted_iota(jnp.int32, (basis_count, LANES), 1)
    sub_small = lax.broadcasted_iota(jnp.int32, (basis_count, LANES), 0)
    for i in range(basis_count):
        total = jnp.zeros((basis_count, LANES), F32)
        for r in range(rows_own):
            piece = basis_ref[:, r * LANES : (r + 1) * LANES]
            total = total + piece * piece[i : i + 1]
        gram = gram + jnp.where(lane_small == 1 + i, jnp.sum(total, axis=1, keepdims=True), 0.0)
    gram_ref[...] = gram

    for k in units:
        arrived(cur_in.at[k - 1], cur_sem.at[0, k - 1], cur_sem.at[1, k - 1])
    row_spot = lax.broadcasted_iota(jnp.int32, (rows_all, leaf_size), 0)
    lane_spot = lax.broadcasted_iota(jnp.int32, (LANES, leaf_size), 0)
    depth = -(-3 * rows_all // LANES) * LANES
    placed_ref[s] = cur_ref[...]
    for k in units:
        placed_ref[sub_of(k)] = cur_in[k - 1]
    pieces = split3(placed_ref[...].reshape(rows_all, LANES))
    pad = [jnp.zeros((depth - 3 * rows_all, LANES), F32)] if depth > 3 * rows_all else []
    stack = jnp.concatenate(list(pieces) + pad, axis=0).T.astype(BF16)

    def hot_rows(order):
        index = jnp.concatenate(order, axis=1)
        return (
            row_spot == lax.shift_right_logical(index, 7),
            lane_spot == lax.bitwise_and(index, LANES - 1),
        )

    def order_of(k, j):
        rows = range(j * groups, (j + 1) * groups)
        if k == 0:
            return [order_ref[r : r + 1, :] for r in rows]
        return [ord_in[k - 1, r : r + 1, :] for r in rows]

    def in_tree_order(k, j):
        in_row, in_lane = hot_rows(order_of(k, j))
        hot = jnp.where(in_row, 1.0, 0.0)
        fill = [jnp.zeros((depth - 3 * rows_all, leaf_size), F32)] if depth > 3 * rows_all else []
        picked = jnp.dot(
            stack, jnp.concatenate([hot] * 3 + fill, axis=0).astype(BF16), preferred_element_type=F32
        )
        return jnp.sum(jnp.where(in_lane, picked, 0.0), axis=0, keepdims=True)

    tree = [in_tree_order(0, j) for j in range(per)]

    def weigh(p, vectors):
        total = jnp.zeros((skel, LANES), F32)
        for j in range(per):
            part = jnp.zeros((skel, LANES), F32)
            for g in range(groups):
                piece = vectors[j][:, g * LANES : (g + 1) * LANES]
                part = part + lmap_ref[j, :, g * LANES : (g + 1) * LANES] * piece
                total = total + rmap_ref[j, :, g * LANES : (g + 1) * LANES] * piece
            vw_ref[p, 0, j : j + 1, 0:leaf_size] = vectors[j]
            vw_ref[p, 0, j : j + 1, leaf_size : leaf_size + skel] = row_of(part)
        vw_ref[p, 0, per : per + 1, 0:skel] = row_of(total)
        for k in units:
            start(
                vw_ref.at[p, 0],
                vw_ref.at[p, inverse(k)],
                vw_sem.at[p, 0, k - 1],
                vw_sem.at[p, 1, inverse(k) - 1],
                (t, sub_of(k)),
            )
        start(
            vw_ref.at[p, 0],
            vw_ref.at[p, halo],
            vw_sem.at[p, 0, halo - 1],
            vw_sem.at[p, 1, halo - 1],
            (prev_leaf, s),
        )

    def near_block(r, c, m1, m2):
        va = None
        if m2 is not None:
            va = [
                vrow_ref[c, :, g * LANES : (g + 1) * LANES] * m2
                for g in range(groups)
            ]
        acc = [jnp.zeros((8, LANES), F32) for _ in range(groups)]
        for m in range(0, leaf_size, CHUNK):
            inner = jnp.dot(row_ref[r, m : m + CHUNK], col_ref[c], preferred_element_type=F32)
            e = jnp.exp2(inner)
            w = vb_ref[r, m : m + CHUNK]
            tot = None
            for g in range(groups):
                piece = e[:, g * LANES : (g + 1) * LANES]
                acc[g] = acc[g] + fold(piece * w)
                if va is not None:
                    q = piece * va[g]
                    tot = q if tot is None else tot + q
            if va is not None:
                acc2_ref[r, m : m + CHUNK] += tot
        for g in range(groups):
            acc1_ref[c, :, g * LANES : (g + 1) * LANES] += acc[g] * m1

    def table_row(table, place, slot):
        return table[place, pl.ds(slot, 1), :]

    def own_pair(r, c, k, j, both=True):
        m1 = table_row(ntab_ref, c, cols + s * per + r)
        m2 = table_row(ntab_ref, r, cols + sub_of(k) * per + j) if both else None
        near_block(r, c, m1, m2)

    def near_diagonal():
        def diagonal(i, carry):
            own_pair(i, i, 0, i, False)
            return carry

        lax.fori_loop(0, per, diagonal, 0, unroll=per)

    def near_own():
        for d in range(1, per // 2 + 1):
            count = per if 2 * d < per else per // 2

            def pair(i, carry):
                j = lax.rem(i + d, per)
                own_pair(i, j, 0, j)
                return carry

            lax.fori_loop(0, count, pair, 0, unroll=count)

    def near_unit(k):
        half = per // 2

        def pair(b, carry):
            o = lax.div(b, half)
            j = 2 * lax.rem(b, half) + lax.rem(o + upper(k), 2)
            own_pair(o, k * per + j, k, j)
            return carry

        lax.fori_loop(0, per * half, pair, 0, unroll=per * half)

    def near_halo(first, last):
        def outer(run, carry):
            i, pair = lax.rem(run, per), lax.div(run, per)

            def step(b, carry):
                c = pair * 2 * per + b
                place = sub_of_dynamic(lax.div(c, per)) * per + lax.rem(c, per)
                m1 = table_row(ntab_ref, c, 2 * cols + s * per + i)
                m2 = table_row(ntab_ref, cols + i, place)
                near_block(per + i, c, m1, m2)
                return carry

            return lax.fori_loop(0, 2 * per, step, carry, unroll=2 * per)

        lax.fori_loop(first, last, outer, 0)

    def far_block(p, r, k, parity):
        inner = jnp.dot(zrow_ref[r], zcol_ref[k], preferred_element_type=F32)
        both = parity is not None or r == 1
        for i in range(per):
            acc, ways = [], []
            for j in range(per):
                peer = (sub_of(k) if r == 0 else sub_of_dynamic(k)) * per + j
                slot = (cols if r == 0 else 2 * cols) + s * per + i
                m1 = table_row(ftab_ref, k * per + j, slot)
                m2 = table_row(ftab_ref, i if r == 0 else cols + i, (cols if r == 0 else 0) + peer)
                if parity is not None:
                    use = (1 - lax.rem(parity + i + j, 2)).astype(F32)
                    m1, m2 = m1 * use, m2 * use
                w = vw_ref[p, k, j : j + 1, leaf_size : leaf_size + skel]
                ways.append((m1, w * m2))
            rows = slice(i * skel, (i + 1) * skel)
            e = jnp.exp2(inner[rows])
            wb = wb_ref[r, rows]
            tot = None
            for j in range(per):
                piece = e[:, j * skel : (j + 1) * skel]
                acc.append(fold(piece * wb))
                if both:
                    q = piece * ways[j][1]
                    tot = q if tot is None else tot + q
            if both:
                fac2_ref[r, rows] += tot
            for j in range(per):
                fac1_ref[k, :, j * skel : (j + 1) * skel] += acc[j] * ways[j][0]

    def spread(p, k):
        for j in range(per):
            value = vw_ref[p, k, j : j + 1, 0:leaf_size]
            if k != halo:
                vrow_ref[k * per + j] = value
            if k in (0, halo):
                r = j if k == 0 else per + j
                vb_ref[r] = column_of(value)
                wb_ref[r // per, j * skel : (j + 1) * skel] = column_of(
                    vw_ref[p, k, j : j + 1, leaf_size : leaf_size + skel]
                )

    def wait_vw(p, k):
        arrived(vw_ref.at[p, k], vw_sem.at[p, 0, k - 1], vw_sem.at[p, 1, k - 1])

    def clear():
        acc1_ref[...] = jnp.zeros_like(acc1_ref)
        acc2_ref[...] = jnp.zeros_like(acc2_ref)
        fac1_ref[...] = jnp.zeros_like(fac1_ref)
        fac2_ref[...] = jnp.zeros_like(fac2_ref)

    home = lax.rem(t, subs)

    def send_root_weights(p):
        total = vw_ref[p, 0, per : per + 1, 0:skel]
        for k in units:
            total = total + vw_ref[p, k, per : per + 1, 0:skel]
        wroot_own[p] = jnp.broadcast_to(total, (8, skel))

        @pl.when(s == home)
        def _():
            for d in range(1, leaves):
                copy(
                    wroot_own.at[p],
                    wroot_in.at[p, lax.div(t, subs)],
                    wroot_send.at[p, d - 1],
                    wroot_recv.at[p, lax.div(t, subs)],
                    (lax.rem(t + d, leaves), s),
                ).start()

    def root_of(q):
        return q * subs + s

    def present(q):
        u = root_of(q)
        return jnp.logical_and(u != t, u < leaves)

    def top(p):
        total = jnp.zeros((8, LANES), F32)
        for q in range(quota):

            @pl.when(present(q))
            def _():
                arrived(wroot_in.at[p, q], wroot_send.at[p, 0], wroot_recv.at[p, q])

            @pl.when(jnp.logical_not(present(q)))
            def _():
                wroot_in[p, q] = jnp.zeros((8, skel), F32)

            column = column_of(wroot_in[p, q, 0:1, :])
            total = total + fold(kroot_ref[q] * column)
        return jnp.sum(total, axis=0, keepdims=True)

    def reduce_halo(p):
        for j in range(per):
            rs_out[p, 0, j : j + 1, 0:leaf_size] = row_of(acc2_ref[per + j])
            rs_out[p, 0, j : j + 1, leaf_size : leaf_size + skel] = row_of(
                fac2_ref[1, j * skel : (j + 1) * skel]
            )
        start(
            rs_out.at[p, 0],
            rs_in.at[p, halo - 1],
            rs_sem.at[p, 0, halo - 1],
            rs_sem.at[p, 1, halo - 1],
            (next_leaf, s),
        )

    def reduce_units(p, root_out):
        for k in units:
            for j in range(per):
                c = k * per + j
                rs_out[p, k, j : j + 1, 0:leaf_size] = jnp.sum(acc1_ref[c], axis=0, keepdims=True)
            rs_out[p, k, 0:per, leaf_size : leaf_size + skel] = jnp.concatenate(
                [
                    jnp.sum(fac1_ref[k, :, j * skel : (j + 1) * skel], axis=0, keepdims=True)
                    for j in range(per)
                ],
                axis=0,
            )
            rs_out[p, k, per : per + 1, 0:skel] = root_out
            start(
                rs_out.at[p, k],
                rs_in.at[p, inverse(k) - 1],
                rs_sem.at[p, 0, k - 1],
                rs_sem.at[p, 1, inverse(k) - 1],
                (t, sub_of(k)),
            )

    def reduce_finish(p, root_out):
        nears, fars = [], []
        for j in range(per):
            nears.append(jnp.sum(acc1_ref[j], axis=0, keepdims=True) + row_of(acc2_ref[j]))
            fars.append(
                jnp.sum(fac1_ref[0, :, j * skel : (j + 1) * skel], axis=0, keepdims=True)
                + row_of(fac2_ref[0, j * skel : (j + 1) * skel])
            )
        for k in range(1, subs + 1):
            arrived(rs_in.at[p, k - 1], rs_sem.at[p, 0, k - 1], rs_sem.at[p, 1, k - 1])
            for j in range(per):
                nears[j] = nears[j] + rs_in[p, k - 1, j : j + 1, 0:leaf_size]
                fars[j] = fars[j] + rs_in[p, k - 1, j : j + 1, leaf_size : leaf_size + skel]
            if k < subs:
                root_out = root_out + rs_in[p, k - 1, per : per + 1, 0:skel]
        root_column = column_of(root_out)
        applied = []
        for j in range(per):
            far_column = column_of(fars[j])
            parts = []
            for g in range(groups):
                lanes = slice(g * LANES, (g + 1) * LANES)
                both = lmap_ref[j, :, lanes] * far_column + rmap_ref[j, :, lanes] * root_column
                parts.append(jnp.sum(both, axis=0, keepdims=True))
            applied.append(nears[j] + jnp.concatenate(parts, axis=1))
        return applied

    weigh(0, tree)
    for j in range(early, per):
        send_points(j)
    send_units(basis_ref, bas_in, bas_sem)
    spread(0, 0)
    for k in units:
        arrived(ord_in.at[k - 1], ord_sem.at[0, k - 1], ord_sem.at[1, k - 1])
        for j in range(per):
            vrow_ref[k * per + j] = in_tree_order(k, j)
    clear()
    near_diagonal()

    def forward(j):
        for k in across:
            arrived(xin_ref.at[k, j], pts_send.at[k, j], pts_recv.at[k, j])
            start(
                xin_ref.at[k, j],
                xin_ref.at[k + 1, j],
                pts_send.at[k + 1, j],
                pts_recv.at[k + 1, j],
                (t, sub_of(sibling)),
            )

    def take_points(k):
        arrived(meta_in.at[k - 1], meta_sem.at[0, k - 1], meta_sem.at[1, k - 1])
        for j in range(per):
            if k not in across:
                arrived(xin_ref.at[k, j], pts_send.at[k, j], pts_recv.at[k, j])
        for j in range(per):
            build_col(k * per + j, xin_ref[k, j])
            build_tables(k, j)
            build_skeleton(k, j, True, None)

    def take_halo(j):
        arrived(xin_ref.at[halo, j], pts_send.at[halo, j], pts_recv.at[halo, j])
        build_row(per + j, xin_ref[halo, j])
        build_tables(halo, j)
        build_skeleton(halo, j, False, per + j)

    forward(0)
    take_points(sibling)
    near_unit(sibling)
    for j in range(1, early):
        forward(j)
    arrived(meta_in.at[halo - 1], meta_sem.at[0, halo - 1], meta_sem.at[1, halo - 1])
    wait_vw(0, halo)
    spread(0, halo)
    for j in range(early):
        take_halo(j)
    near_halo(0, early)
    for j in range(early, per):
        forward(j)
    for k in units:
        if k != sibling:
            take_points(k)
            near_unit(k)

    root_points = jnp.zeros((4 * feat, skel), F32)
    for k in range(subs):
        for j in range(per):
            base = (sub_of(k) * per + j) * leaf_size
            chosen = one_hot(rskel_ref[...] - base)
            root_points = root_points + jnp.dot(
                col_ref[k * per + j], chosen.astype(BF16), preferred_element_type=F32
            )
    rcol_ref[...] = root_points.astype(BF16)
    root_own[...] = root_points[0:feat] + root_points[2 * feat : 3 * feat]

    @pl.when(s == home)
    def _():
        for d in range(1, leaves):
            copy(
                root_own,
                root_in.at[lax.div(t, subs)],
                root_send.at[d - 1],
                root_recv.at[lax.div(t, subs)],
                (lax.rem(t + d, leaves), s),
            ).start()

    for k in units:
        wait_vw(0, k)
    send_root_weights(0)
    for j in range(early, per):
        take_halo(j)
    near_halo(early, per * chips)

    def far_halo(p):
        def step(k, carry):
            far_block(p, 1, k, None)
            return carry

        lax.fori_loop(0, subs, step, 0)

    def far_units(p):
        for k in units:
            far_block(p, 0, k, upper(k))

    far_halo(0)
    reduce_halo(0)
    far_units(0)
    for q in range(quota):

        @pl.when(present(q))
        def _():
            arrived(root_in.at[q], root_send.at[0], root_recv.at[q])

        @pl.when(jnp.logical_not(present(q)))
        def _():
            root_in[q] = root_own[...]

        rows = jnp.concatenate(augmented(root_in[q], scale, True), axis=0).T.astype(BF16)
        kroot_ref[q] = jnp.exp2(jnp.dot(rows, rcol_ref[...], preferred_element_type=F32))

    root_out = top(0)
    reduce_units(0, root_out)
    near_own()
    far_block(0, 0, 0, None)
    applied = reduce_finish(0, root_out)
    first = [tree[j] - (applied[j] + RIDGE_SHIFT * tree[j]) / ritz_ref[0] for j in range(per)]

    weigh(1, first)
    spread(1, 0)
    clear()
    near_diagonal()
    for k in units:
        wait_vw(1, k)
        spread(1, k)
    wait_vw(1, halo)
    spread(1, halo)
    send_root_weights(1)
    near_halo(0, per * chips)
    far_halo(1)
    reduce_halo(1)
    for k in units:
        near_unit(k)
    far_units(1)
    root_out = top(1)
    reduce_units(1, root_out)
    near_own()
    far_block(1, 0, 0, None)
    applied = reduce_finish(1, root_out)
    square = jnp.zeros((1, leaf_size), F32)
    placed = jnp.zeros((rows_all, LANES), F32)
    for j in range(per):
        v0 = vw_ref[0, 0, j : j + 1, 0:leaf_size]
        v1 = vw_ref[1, 0, j : j + 1, 0:leaf_size]
        second = v1 - (applied[j] + RIDGE_SHIFT * v1) / ritz_ref[1]
        grown = v0 - second
        square = square + grown * grown
        in_row, in_lane = hot_rows(order_of(0, j))
        held = jnp.concatenate(split3(jnp.where(in_row, grown, 0.0)), axis=0)
        hot = jnp.where(in_lane, 1.0, 0.0).astype(BF16)
        spots = lax.dot_general(
            held.astype(BF16), hot, (((1,), (1,)), ((), ())), preferred_element_type=F32
        )
        placed = placed + (
            spots[0:rows_all] + spots[rows_all : 2 * rows_all] + spots[2 * rows_all : 3 * rows_all]
        )
    placed_ref[...] = placed.reshape(subs, rows_own, LANES)
    for k in units:
        start(
            placed_ref.at[sub_of(k)],
            fin_in.at[inverse(k) - 1],
            fin_sem.at[0, k - 1],
            fin_sem.at[1, inverse(k) - 1],
            (t, sub_of(k)),
        )

    part = jnp.zeros((basis_count, LANES), F32)
    for k in range(subs):
        if k:
            arrived(bas_in.at[k - 1], bas_sem.at[0, k - 1], bas_sem.at[1, k - 1])
        spots = placed_ref[sub_of(k)]
        for r in range(rows_own):
            lanes = slice(r * LANES, (r + 1) * LANES)
            piece = basis_ref[:, lanes] if k == 0 else bas_in[k - 1, :, lanes]
            part = part + piece * spots[r : r + 1]
    corner = jnp.logical_and(lane_small == 1 + basis_count, sub_small == 0)
    tot_own[...] = (
        gram_ref[...]
        + jnp.where(lane_small == 0, jnp.sum(part, axis=1, keepdims=True), 0.0)
        + jnp.where(corner, jnp.sum(square, axis=1, keepdims=True), 0.0)
    )
    send_units(tot_own, tot_in, tots_sem)
    for k in units:
        arrived(tot_in.at[k - 1], tots_sem.at[0, k - 1], tots_sem.at[1, k - 1])
    tot_all[0] = tot_own[...]
    for k in units:
        tot_all[k] = tot_in[k - 1]
    total = tot_all[sub_order(chip, core, 0, chips)]
    for i in range(1, subs):
        total = total + tot_all[sub_order(chip, core, i, chips)]
    tot_sub[t] = total
    for d in range(1, leaves):
        start(
            tot_sub.at[t],
            tot_sub.at[t],
            totl_sem.at[0, d - 1],
            totl_sem.at[1, d - 1],
            (lax.rem(t + d, leaves), s),
        )
    user = placed_ref[s]
    for k in units:
        arrived(fin_in.at[k - 1], fin_sem.at[0, k - 1], fin_sem.at[1, k - 1])
        user = user + fin_in[k - 1]
    for d in range(1, leaves):
        slot = tot_sub.at[lax.rem(t + leaves - d, leaves)]
        arrived(slot, totl_sem.at[0, d - 1], totl_sem.at[1, d - 1])
    total = tot_sub[0]
    for u in range(1, leaves):
        total = total + tot_sub[u]
    proj = total[:, 0:1]
    squares = jnp.sum(jnp.where(corner, total, 0.0), keepdims=True)
    proj_row = jnp.sum(jnp.where(lane_small == 1 + sub_small, proj, 0.0), axis=0, keepdims=True)
    gram_proj = jnp.sum(
        jnp.where(jnp.logical_and(lane_small >= 1, lane_small <= basis_count), total, 0.0) * proj_row,
        axis=1,
        keepdims=True,
    )
    length_sq = (
        squares
        - 2.0 * jnp.sum(proj * proj, axis=0, keepdims=True)
        + jnp.sum(proj * gram_proj, axis=0, keepdims=True)
    )
    norm = jnp.sqrt(length_sq + EPSILON)
    hess = jnp.sum(jnp.where(lane_small == sub_small, proj, 0.0), axis=0, keepdims=True)
    hess_ref[...] = hess + jnp.where(lane_small[0:1] == basis_count, norm, 0.0)
    for r in range(rows_own):
        span = jnp.sum(basis_ref[:, r * LANES : (r + 1) * LANES] * proj, axis=0, keepdims=True)
        orth_ref[r : r + 1] = user[r : r + 1] - span

    for c in started:
        c.wait_send()

    @pl.when(s == home)
    def _():
        there = (next_leaf, s)
        for d in range(1, leaves):
            q = lax.div(t, subs)
            copy(root_own, root_in.at[q], root_send.at[d - 1], root_recv.at[q], there).wait_send()
            for p in range(2):
                copy(
                    wroot_own.at[p], wroot_in.at[p, q], wroot_send.at[p, d - 1], wroot_recv.at[p, q], there
                ).wait_send()


def sub_order(chip, core, i, chips):
    return lax.rem(i // 2 + chips - chip, chips) * 2 + lax.rem(i % 2 + 2 - core, 2)


def shards(
    points,
    leaf_maps,
    root_maps,
    current,
    krylov_basis,
    ritz_roots,
    point_order,
    skeleton,
    root_skeleton,
    near_list,
    far_list,
):
    per, skel, leaf_size = leaf_maps.shape
    feat = points.shape[1]
    subs, leaves = lax.axis_size("sub"), lax.axis_size("leaf")
    near_count, far_count = near_list.shape[1], far_list.shape[1]
    basis_count = krylov_basis.shape[0]
    dims = (per, leaf_size, feat, skel, leaves, subs, near_count, far_count, basis_count)
    cols, rows_own = per * subs, per * leaf_size // LANES
    quota = -(-leaves // subs)
    xt = points.reshape(per, leaf_size, feat).transpose(0, 2, 1)
    wide = leaf_size + skel
    dma = pltpu.SemaphoreType.DMA
    scratch = [
        pltpu.VMEM((subs + 1, per, feat, leaf_size), F32),
        pltpu.VMEM((per, leaf_size), F32),
        pltpu.VMEM((subs, per, leaf_size), F32),
        pltpu.VMEM((subs - 1, rows_own, LANES), F32),
        pltpu.VMEM((subs - 1, rows_own, LANES), jnp.int32),
        pltpu.VMEM((subs - 1, basis_count, rows_own * LANES), F32),
        pltpu.VMEM((cols, 4 * feat, leaf_size), BF16),
        pltpu.VMEM((2 * per, leaf_size, 4 * feat), BF16),
        pltpu.VMEM((subs, 4 * feat, per * skel), BF16),
        pltpu.VMEM((2, per * skel, 4 * feat), BF16),
        pltpu.VMEM((cols + per, 3 * cols, LANES), F32),
        pltpu.VMEM((cols + per, 3 * cols, LANES), F32),
        pltpu.VMEM((2, subs + 1, 2 * per, wide), F32),
        pltpu.VMEM((cols, 1, leaf_size), F32),
        pltpu.VMEM((2 * per, leaf_size, LANES), F32),
        pltpu.VMEM((2, per * skel, LANES), F32),
        pltpu.VMEM((cols, 8, leaf_size), F32),
        pltpu.VMEM((2 * per, leaf_size, LANES), F32),
        pltpu.VMEM((subs, 8, per * skel), F32),
        pltpu.VMEM((2, per * skel, LANES), F32),
        pltpu.VMEM((feat, skel), F32),
        pltpu.VMEM((quota, feat, skel), F32),
        pltpu.VMEM((4 * feat, skel), BF16),
        pltpu.VMEM((quota, skel, LANES), F32),
        pltpu.VMEM((2, 8, skel), F32),
        pltpu.VMEM((2, quota, 8, skel), F32),
        pltpu.VMEM((2, subs, 2 * per, wide), F32),
        pltpu.VMEM((2, subs, 2 * per, wide), F32),
        pltpu.VMEM((subs, rows_own, LANES), F32),
        pltpu.VMEM((subs - 1, rows_own, LANES), F32),
        pltpu.VMEM((basis_count, LANES), F32),
        pltpu.VMEM((subs - 1, basis_count, LANES), F32),
        pltpu.VMEM((leaves, basis_count, LANES), F32),
        pltpu.VMEM((subs, basis_count, LANES), F32),
        pltpu.VMEM((basis_count, LANES), F32),
        dma((2, subs - 1)),
        dma((2, subs - 1)),
        dma((2, subs - 1)),
        dma((2, subs)),
        dma((subs + 1, per)),
        dma((subs + 1, per)),
        dma((2, 2, subs)),
        dma((2, 2, subs)),
        dma((leaves - 1,)),
        dma((quota,)),
        dma((2, leaves - 1)),
        dma((2, quota)),
        dma((2, subs - 1)),
        dma((2, subs - 1)),
        dma((2, leaves - 1)),
    ]
    orth, hess = pl.pallas_call(
        lambda *refs: kernel_body(dims, *refs),
        out_shape=[
            jax.ShapeDtypeStruct((rows_own, LANES), F32),
            jax.ShapeDtypeStruct((1, LANES), F32),
        ],
        in_specs=[VMEM] * 10 + [SMEM],
        out_specs=[VMEM] * 2,
        scratch_shapes=scratch,
        compiler_params=pltpu.CompilerParams(
            collective_id=0, has_side_effects=True, vmem_limit_bytes=48 * 1024 * 1024
        ),
        name="step",
    )(
        xt,
        leaf_maps,
        root_maps,
        current.reshape(rows_own, LANES),
        point_order.reshape(rows_own, LANES),
        skeleton,
        root_skeleton,
        near_list,
        far_list,
        krylov_basis,
        ritz_roots,
    )
    return orth.reshape(-1), hess[0, : basis_count + 1]


def solution(mesh):
    return jax.shard_map(
        shards,
        mesh=mesh,
        in_specs=(
            P(("leaf", "sub"), None),
            P(("leaf", "sub"), None, None),
            P(("leaf", "sub"), None, None),
            P(("leaf", "sub")),
            P(None, ("leaf", "sub")),
            P(),
            P(("leaf", "sub")),
            P(("leaf", "sub"), None),
            P("leaf", None),
            P(("leaf", "sub"), None),
            P(("leaf", "sub"), None),
        ),
        out_specs=(P(("leaf", "sub")), P()),
        check_vma=False,
    )
```

```python
import jax
import jax.numpy as jnp
from jax import lax
from jax.experimental import pallas as pl
from jax.experimental.pallas import tpu as pltpu
from jax.sharding import PartitionSpec as P

RIDGE_SHIFT = 1.0
EPSILON = 1e-06
LOG2E = 1.4426950408889634
LANES = 128
CHUNK = 512
MESH = pl.DeviceIdType.MESH
VMEM = pl.BlockSpec(memory_space=pltpu.VMEM)
ANY = pl.BlockSpec(memory_space=pl.ANY)
SMEM = pl.BlockSpec(memory_space=pltpu.SMEM)
F32, BF16 = jnp.float32, jnp.bfloat16


def bf16_part(x):
    return x.astype(BF16).astype(F32)


def augmented(x, scale, target):
    feat, size = x.shape
    sq = -scale * jnp.sum(x * x, axis=0, keepdims=True)
    s1 = bf16_part(sq)
    s2 = bf16_part(sq - s1)
    s3 = sq - s1 - s2
    row = lax.broadcasted_iota(jnp.int32, (feat, size), 0)
    first = 3 if target else 0
    ones = jnp.where(row < 6, 1.0, 0.0)
    extra = jnp.where(
        row == first,
        s1,
        jnp.where(row == first + 1, s2, jnp.where(row == first + 2, s3, ones)),
    )
    if target:
        x = x * (2.0 * scale)
    hi = bf16_part(x)
    lo = x - hi
    return (hi, lo, hi, extra) if target else (hi, hi, lo, extra)


def split3(x):
    hi = bf16_part(x)
    mid = bf16_part(x - hi)
    return hi, mid, x - hi - mid


def column_of(row):
    return jnp.broadcast_to(row, (LANES, row.shape[1])).T


def fold(block):
    return jnp.sum(block.reshape(block.shape[0] // 8, 8, LANES), axis=0)


def row_of(block):
    return jnp.sum(block.T, axis=0, keepdims=True)


def kernel_body(dims, *refs):
    (per, leaf_size, feat, skel, leaves, subs, near_count, far_count, basis_count) = dims
    (
        points_any,
        lmap_any,
        rmap_any,
        cur_ref,
        order_ref,
        skel_ref,
        rskel_ref,
        near_ref,
        far_ref,
        basis_any,
        ritz_ref,
        orth_ref,
        hess_ref,
        raw_ref,
        xt_ref,
        lmap_ref,
        rmap_ref,
        basis_ref,
        xin_ref,
        meta_own,
        meta_in,
        cur_in,
        ord_in,
        bas_in,
        col_ref,
        row_ref,
        zcol_ref,
        zrow_ref,
        ntab_ref,
        ftab_ref,
        vw_ref,
        vrow_ref,
        vb_ref,
        wb_ref,
        acc1_ref,
        acc2_ref,
        fac1_ref,
        fac2_ref,
        root_own,
        root_in,
        rcol_ref,
        kroot_ref,
        wroot_own,
        wroot_in,
        rs_out,
        rs_in,
        placed_ref,
        fin_in,
        tot_own,
        tot_in,
        tot_sub,
        tot_all,
        gram_ref,
        load_sem,
        cur_sem,
        ord_sem,
        bas_sem,
        meta_sem,
        pts_send,
        pts_recv,
        vw_sem,
        rs_sem,
        root_send,
        root_recv,
        wroot_send,
        wroot_recv,
        fin_sem,
        tots_sem,
        totl_sem,
    ) = refs
    t, s = lax.axis_index("leaf"), lax.axis_index("sub")
    chips = subs // 2
    chip, core = lax.div(s, 2), lax.rem(s, 2)
    cols = per * subs
    groups = leaf_size // LANES
    rows_own = per * leaf_size // LANES
    rows_all = subs * rows_own
    scale = LOG2E / feat
    halo = subs
    quota = -(-leaves // subs)
    next_leaf, prev_leaf = lax.rem(t + 1, leaves), lax.rem(t + leaves - 1, leaves)
    units = range(1, subs)

    def sub_of(k):
        return lax.rem(chip + k // 2, chips) * 2 + lax.rem(core + k % 2, 2)

    def sub_of_dynamic(k):
        return lax.rem(chip + lax.div(k, 2), chips) * 2 + lax.rem(core + lax.rem(k, 2), 2)

    def inverse(k):
        return (chips - k // 2) % chips * 2 + k % 2

    def upper(k):
        return lax.div(s - sub_of(k) + subs - 1, subs)

    def copy(src, dst, send, recv, there):
        return pltpu.make_async_remote_copy(
            src_ref=src, dst_ref=dst, send_sem=send, recv_sem=recv, device_id=there, device_id_type=MESH
        )

    started = []

    def start(*args):
        c = copy(*args)
        c.start()
        started.append(c)

    def arrived(dst, send, recv):
        copy(dst, dst, send, recv, (t, sub_of(1))).wait_recv()

    barrier = pltpu.get_barrier_semaphore()
    peers = [(lax.rem(t + d, leaves), s) for d in range(1, leaves)]
    peers += [(t, sub_of(k)) for k in units]
    for there in peers:
        pl.semaphore_signal(barrier, inc=1, device_id=there, device_id_type=MESH)

    loads = [
        pltpu.make_async_copy(src, dst, load_sem.at[i])
        for i, (src, dst) in enumerate(
            (
                (points_any, raw_ref),
                (basis_any, basis_ref),
                (lmap_any, lmap_ref),
                (rmap_any, rmap_ref),
            )
        )
    ]
    for c in loads:
        c.start()

    meta_own[...] = jnp.zeros_like(meta_own)
    meta_own[:, 0:skel] = skel_ref[...].astype(F32)
    meta_own[:, LANES : LANES + near_count] = near_ref[...].astype(F32)
    meta_own[:, 2 * LANES : 2 * LANES + far_count] = far_ref[...].astype(F32)
    def build_col(c, x):
        for i, piece in enumerate(augmented(x, scale, False)):
            col_ref[c, i * feat : (i + 1) * feat] = piece.astype(BF16)

    def build_row(r, x):
        pieces = augmented(x, scale, True)
        row_ref[r] = jnp.concatenate(pieces, axis=0).T.astype(BF16)

    def one_hot(index_row):
        spot = lax.broadcasted_iota(jnp.int32, (leaf_size, skel), 0)
        return jnp.where(spot == index_row, 1.0, 0.0)

    def meta_row(k, j, lane, count):
        if k == 0:
            return meta_own[j : j + 1, lane : lane + count]
        return meta_in[k - 1, j : j + 1, lane : lane + count]

    def build_tables(k, j):
        place = k * per + j
        slots = lax.broadcasted_iota(jnp.int32, (3 * cols, 1), 0).astype(F32)
        for table, lane, count in ((ntab_ref, LANES, near_count), (ftab_ref, 2 * LANES, far_count)):
            hit = jnp.where(slots == meta_row(k, j, lane, count), 1.0, 0.0)
            table[place] = jnp.broadcast_to(jnp.max(hit, axis=1, keepdims=True), (3 * cols, LANES))

    def build_skeleton(k, j, as_col, r):
        chosen = one_hot(meta_row(k, j, 0, skel).astype(jnp.int32))
        if as_col:
            picked = jnp.dot(col_ref[k * per + j], chosen.astype(BF16), preferred_element_type=F32)
            zcol_ref[k, :, j * skel : (j + 1) * skel] = picked.astype(BF16)
        if r is not None:
            picked = jnp.dot(chosen.T.astype(BF16), row_ref[r], preferred_element_type=F32)
            zrow_ref[r // per, j * skel : (j + 1) * skel, :] = picked.astype(BF16)

    loads[0].wait()
    for j in range(per):
        xt_ref[j] = raw_ref[j * leaf_size : (j + 1) * leaf_size, :].T
        build_col(j, xt_ref[j])
        build_row(j, xt_ref[j])
    for j in range(per):
        build_tables(0, j)
        build_skeleton(0, j, True, j)
    loads[1].wait()
    gram = jnp.zeros((basis_count, LANES), F32)
    lane_small = lax.broadcasted_iota(jnp.int32, (basis_count, LANES), 1)
    sub_small = lax.broadcasted_iota(jnp.int32, (basis_count, LANES), 0)
    for i in range(basis_count):
        total = jnp.zeros((basis_count, LANES), F32)
        for r in range(rows_own):
            piece = basis_ref[:, r * LANES : (r + 1) * LANES]
            total = total + piece * piece[i : i + 1]
        gram = gram + jnp.where(lane_small == 1 + i, jnp.sum(total, axis=1, keepdims=True), 0.0)
    gram_ref[...] = gram

    pl.semaphore_wait(barrier, len(peers))
    def send_units(src, dst, sem):
        for k in units:
            start(src, dst.at[inverse(k) - 1], sem.at[0, k - 1], sem.at[1, inverse(k) - 1], (t, sub_of(k)))

    across = [k for k in units if k % 2 == 0]
    sibling = 1

    def send_points(j):
        to = [(k, inverse(k), (t, sub_of(k))) for k in across]
        to += [(halo, halo, (prev_leaf, s)), (sibling, sibling, (t, sub_of(sibling)))]
        for k, slot, there in to:
            start(xt_ref.at[j], xin_ref.at[slot, j], pts_send.at[k, j], pts_recv.at[slot, j], there)

    early = per // 2
    send_units(cur_ref, cur_in, cur_sem)
    send_units(order_ref, ord_in, ord_sem)
    send_units(meta_own, meta_in, meta_sem)
    start(meta_own, meta_in.at[halo - 1], meta_sem.at[0, halo - 1], meta_sem.at[1, halo - 1], (prev_leaf, s))
    for j in range(early):
        send_points(j)

    for k in units:
        arrived(cur_in.at[k - 1], cur_sem.at[0, k - 1], cur_sem.at[1, k - 1])
    row_spot = lax.broadcasted_iota(jnp.int32, (rows_all, leaf_size), 0)
    lane_spot = lax.broadcasted_iota(jnp.int32, (LANES, leaf_size), 0)
    depth = -(-3 * rows_all // LANES) * LANES
    placed_ref[s] = cur_ref[...]
    for k in units:
        placed_ref[sub_of(k)] = cur_in[k - 1]
    pieces = split3(placed_ref[...].reshape(rows_all, LANES))
    pad = [jnp.zeros((depth - 3 * rows_all, LANES), F32)] if depth > 3 * rows_all else []
    stack = jnp.concatenate(list(pieces) + pad, axis=0).T.astype(BF16)

    def hot_rows(order):
        index = jnp.concatenate(order, axis=1)
        return (
            row_spot == lax.shift_right_logical(index, 7),
            lane_spot == lax.bitwise_and(index, LANES - 1),
        )

    def order_of(k, j):
        rows = range(j * groups, (j + 1) * groups)
        if k == 0:
            return [order_ref[r : r + 1, :] for r in rows]
        return [ord_in[k - 1, r : r + 1, :] for r in rows]

    def in_tree_order(k, j):
        in_row, in_lane = hot_rows(order_of(k, j))
        hot = jnp.where(in_row, 1.0, 0.0)
        fill = [jnp.zeros((depth - 3 * rows_all, leaf_size), F32)] if depth > 3 * rows_all else []
        picked = jnp.dot(
            stack, jnp.concatenate([hot] * 3 + fill, axis=0).astype(BF16), preferred_element_type=F32
        )
        return jnp.sum(jnp.where(in_lane, picked, 0.0), axis=0, keepdims=True)

    tree = [in_tree_order(0, j) for j in range(per)]

    def weigh(p, vectors):
        total = jnp.zeros((skel, LANES), F32)
        for j in range(per):
            part = jnp.zeros((skel, LANES), F32)
            for g in range(groups):
                piece = vectors[j][:, g * LANES : (g + 1) * LANES]
                part = part + lmap_ref[j, :, g * LANES : (g + 1) * LANES] * piece
                total = total + rmap_ref[j, :, g * LANES : (g + 1) * LANES] * piece
            vw_ref[p, 0, j : j + 1, 0:leaf_size] = vectors[j]
            vw_ref[p, 0, j : j + 1, leaf_size : leaf_size + skel] = row_of(part)
        vw_ref[p, 0, per : per + 1, 0:skel] = row_of(total)
        for k in units:
            start(
                vw_ref.at[p, 0],
                vw_ref.at[p, inverse(k)],
                vw_sem.at[p, 0, k - 1],
                vw_sem.at[p, 1, inverse(k) - 1],
                (t, sub_of(k)),
            )
        start(
            vw_ref.at[p, 0],
            vw_ref.at[p, halo],
            vw_sem.at[p, 0, halo - 1],
            vw_sem.at[p, 1, halo - 1],
            (prev_leaf, s),
        )

    def near_block(r, c, m1, m2):
        va = None
        if m2 is not None:
            va = [
                vrow_ref[c, :, g * LANES : (g + 1) * LANES] * m2
                for g in range(groups)
            ]
        acc = [jnp.zeros((8, LANES), F32) for _ in range(groups)]
        for m in range(0, leaf_size, CHUNK):
            inner = jnp.dot(row_ref[r, m : m + CHUNK], col_ref[c], preferred_element_type=F32)
            e = jnp.exp2(inner)
            w = vb_ref[r, m : m + CHUNK]
            tot = None
            for g in range(groups):
                piece = e[:, g * LANES : (g + 1) * LANES]
                acc[g] = acc[g] + fold(piece * w)
                if va is not None:
                    q = piece * va[g]
                    tot = q if tot is None else tot + q
            if va is not None:
                acc2_ref[r, m : m + CHUNK] += tot
        for g in range(groups):
            acc1_ref[c, :, g * LANES : (g + 1) * LANES] += acc[g] * m1

    def table_row(table, place, slot):
        return table[place, pl.ds(slot, 1), :]

    def own_pair(r, c, k, j, both=True):
        m1 = table_row(ntab_ref, c, cols + s * per + r)
        m2 = table_row(ntab_ref, r, cols + sub_of(k) * per + j) if both else None
        near_block(r, c, m1, m2)

    def near_diagonal():
        def diagonal(i, carry):
            own_pair(i, i, 0, i, False)
            return carry

        lax.fori_loop(0, per, diagonal, 0, unroll=per)

    def near_own():
        for d in range(1, per // 2 + 1):
            count = per if 2 * d < per else per // 2

            def pair(i, carry):
                j = lax.rem(i + d, per)
                own_pair(i, j, 0, j)
                return carry

            lax.fori_loop(0, count, pair, 0, unroll=count)

    def near_unit(k):
        half = per // 2

        def pair(b, carry):
            o = lax.div(b, half)
            j = 2 * lax.rem(b, half) + lax.rem(o + upper(k), 2)
            own_pair(o, k * per + j, k, j)
            return carry

        lax.fori_loop(0, per * half, pair, 0, unroll=per * half)

    def near_halo(first, last):
        def outer(run, carry):
            i, pair = lax.rem(run, per), lax.div(run, per)

            def step(b, carry):
                c = pair * 2 * per + b
                place = sub_of_dynamic(lax.div(c, per)) * per + lax.rem(c, per)
                m1 = table_row(ntab_ref, c, 2 * cols + s * per + i)
                m2 = table_row(ntab_ref, cols + i, place)
                near_block(per + i, c, m1, m2)
                return carry

            return lax.fori_loop(0, 2 * per, step, carry, unroll=2 * per)

        lax.fori_loop(first, last, outer, 0)

    def far_block(p, r, k, parity):
        inner = jnp.dot(zrow_ref[r], zcol_ref[k], preferred_element_type=F32)
        both = parity is not None or r == 1
        for i in range(per):
            acc, ways = [], []
            for j in range(per):
                peer = (sub_of(k) if r == 0 else sub_of_dynamic(k)) * per + j
                slot = (cols if r == 0 else 2 * cols) + s * per + i
                m1 = table_row(ftab_ref, k * per + j, slot)
                m2 = table_row(ftab_ref, i if r == 0 else cols + i, (cols if r == 0 else 0) + peer)
                if parity is not None:
                    use = (1 - lax.rem(parity + i + j, 2)).astype(F32)
                    m1, m2 = m1 * use, m2 * use
                w = vw_ref[p, k, j : j + 1, leaf_size : leaf_size + skel]
                ways.append((m1, w * m2))
            rows = slice(i * skel, (i + 1) * skel)
            e = jnp.exp2(inner[rows])
            wb = wb_ref[r, rows]
            tot = None
            for j in range(per):
                piece = e[:, j * skel : (j + 1) * skel]
                acc.append(fold(piece * wb))
                if both:
                    q = piece * ways[j][1]
                    tot = q if tot is None else tot + q
            if both:
                fac2_ref[r, rows] += tot
            for j in range(per):
                fac1_ref[k, :, j * skel : (j + 1) * skel] += acc[j] * ways[j][0]

    def spread(p, k):
        for j in range(per):
            value = vw_ref[p, k, j : j + 1, 0:leaf_size]
            if k != halo:
                vrow_ref[k * per + j] = value
            if k in (0, halo):
                r = j if k == 0 else per + j
                vb_ref[r] = column_of(value)
                wb_ref[r // per, j * skel : (j + 1) * skel] = column_of(
                    vw_ref[p, k, j : j + 1, leaf_size : leaf_size + skel]
                )

    def wait_vw(p, k):
        arrived(vw_ref.at[p, k], vw_sem.at[p, 0, k - 1], vw_sem.at[p, 1, k - 1])

    def clear():
        acc1_ref[...] = jnp.zeros_like(acc1_ref)
        acc2_ref[...] = jnp.zeros_like(acc2_ref)
        fac1_ref[...] = jnp.zeros_like(fac1_ref)
        fac2_ref[...] = jnp.zeros_like(fac2_ref)

    home = lax.rem(t, subs)

    def send_root_weights(p):
        total = vw_ref[p, 0, per : per + 1, 0:skel]
        for k in units:
            total = total + vw_ref[p, k, per : per + 1, 0:skel]
        wroot_own[p] = jnp.broadcast_to(total, (8, skel))

        @pl.when(s == home)
        def _():
            for d in range(1, leaves):
                copy(
                    wroot_own.at[p],
                    wroot_in.at[p, lax.div(t, subs)],
                    wroot_send.at[p, d - 1],
                    wroot_recv.at[p, lax.div(t, subs)],
                    (lax.rem(t + d, leaves), s),
                ).start()

    def root_of(q):
        return q * subs + s

    def present(q):
        u = root_of(q)
        return jnp.logical_and(u != t, u < leaves)

    def top(p):
        total = jnp.zeros((8, LANES), F32)
        for q in range(quota):

            @pl.when(present(q))
            def _():
                arrived(wroot_in.at[p, q], wroot_send.at[p, 0], wroot_recv.at[p, q])

            @pl.when(jnp.logical_not(present(q)))
            def _():
                wroot_in[p, q] = jnp.zeros((8, skel), F32)

            column = column_of(wroot_in[p, q, 0:1, :])
            total = total + fold(kroot_ref[q] * column)
        return jnp.sum(total, axis=0, keepdims=True)

    def reduce_halo(p):
        for j in range(per):
            rs_out[p, 0, j : j + 1, 0:leaf_size] = row_of(acc2_ref[per + j])
            rs_out[p, 0, j : j + 1, leaf_size : leaf_size + skel] = row_of(
                fac2_ref[1, j * skel : (j + 1) * skel]
            )
        start(
            rs_out.at[p, 0],
            rs_in.at[p, halo - 1],
            rs_sem.at[p, 0, halo - 1],
            rs_sem.at[p, 1, halo - 1],
            (next_leaf, s),
        )

    def reduce_units(p, root_out):
        for k in units:
            for j in range(per):
                c = k * per + j
                rs_out[p, k, j : j + 1, 0:leaf_size] = jnp.sum(acc1_ref[c], axis=0, keepdims=True)
            rs_out[p, k, 0:per, leaf_size : leaf_size + skel] = jnp.concatenate(
                [
                    jnp.sum(fac1_ref[k, :, j * skel : (j + 1) * skel], axis=0, keepdims=True)
                    for j in range(per)
                ],
                axis=0,
            )
            rs_out[p, k, per : per + 1, 0:skel] = root_out
            start(
                rs_out.at[p, k],
                rs_in.at[p, inverse(k) - 1],
                rs_sem.at[p, 0, k - 1],
                rs_sem.at[p, 1, inverse(k) - 1],
                (t, sub_of(k)),
            )

    def reduce_finish(p, root_out):
        nears, fars = [], []
        for j in range(per):
            nears.append(jnp.sum(acc1_ref[j], axis=0, keepdims=True) + row_of(acc2_ref[j]))
            fars.append(
                jnp.sum(fac1_ref[0, :, j * skel : (j + 1) * skel], axis=0, keepdims=True)
                + row_of(fac2_ref[0, j * skel : (j + 1) * skel])
            )
        for k in range(1, subs + 1):
            arrived(rs_in.at[p, k - 1], rs_sem.at[p, 0, k - 1], rs_sem.at[p, 1, k - 1])
            for j in range(per):
                nears[j] = nears[j] + rs_in[p, k - 1, j : j + 1, 0:leaf_size]
                fars[j] = fars[j] + rs_in[p, k - 1, j : j + 1, leaf_size : leaf_size + skel]
            if k < subs:
                root_out = root_out + rs_in[p, k - 1, per : per + 1, 0:skel]
        root_column = column_of(root_out)
        applied = []
        for j in range(per):
            far_column = column_of(fars[j])
            parts = []
            for g in range(groups):
                lanes = slice(g * LANES, (g + 1) * LANES)
                both = lmap_ref[j, :, lanes] * far_column + rmap_ref[j, :, lanes] * root_column
                parts.append(jnp.sum(both, axis=0, keepdims=True))
            applied.append(nears[j] + jnp.concatenate(parts, axis=1))
        return applied

    loads[2].wait()
    loads[3].wait()
    weigh(0, tree)
    for j in range(early, per):
        send_points(j)
    send_units(basis_ref, bas_in, bas_sem)
    spread(0, 0)
    for k in units:
        arrived(ord_in.at[k - 1], ord_sem.at[0, k - 1], ord_sem.at[1, k - 1])
        for j in range(per):
            vrow_ref[k * per + j] = in_tree_order(k, j)
    clear()
    near_diagonal()

    def forward(j):
        for k in across:
            arrived(xin_ref.at[k, j], pts_send.at[k, j], pts_recv.at[k, j])
            start(
                xin_ref.at[k, j],
                xin_ref.at[k + 1, j],
                pts_send.at[k + 1, j],
                pts_recv.at[k + 1, j],
                (t, sub_of(sibling)),
            )

    def take_points(k):
        arrived(meta_in.at[k - 1], meta_sem.at[0, k - 1], meta_sem.at[1, k - 1])
        for j in range(per):
            if k not in across:
                arrived(xin_ref.at[k, j], pts_send.at[k, j], pts_recv.at[k, j])
        for j in range(per):
            build_col(k * per + j, xin_ref[k, j])
            build_tables(k, j)
            build_skeleton(k, j, True, None)

    def take_halo(j):
        arrived(xin_ref.at[halo, j], pts_send.at[halo, j], pts_recv.at[halo, j])
        build_row(per + j, xin_ref[halo, j])
        build_tables(halo, j)
        build_skeleton(halo, j, False, per + j)

    forward(0)
    take_points(sibling)
    near_unit(sibling)
    for j in range(1, early):
        forward(j)
    arrived(meta_in.at[halo - 1], meta_sem.at[0, halo - 1], meta_sem.at[1, halo - 1])
    wait_vw(0, halo)
    spread(0, halo)
    for j in range(early):
        take_halo(j)
    near_halo(0, early)
    for j in range(early, per):
        forward(j)
    for k in units:
        if k != sibling:
            take_points(k)
            near_unit(k)

    root_points = jnp.zeros((4 * feat, skel), F32)
    for k in range(subs):
        for j in range(per):
            base = (sub_of(k) * per + j) * leaf_size
            chosen = one_hot(rskel_ref[...] - base)
            root_points = root_points + jnp.dot(
                col_ref[k * per + j], chosen.astype(BF16), preferred_element_type=F32
            )
    rcol_ref[...] = root_points.astype(BF16)
    root_own[...] = root_points[0:feat] + root_points[2 * feat : 3 * feat]

    @pl.when(s == home)
    def _():
        for d in range(1, leaves):
            copy(
                root_own,
                root_in.at[lax.div(t, subs)],
                root_send.at[d - 1],
                root_recv.at[lax.div(t, subs)],
                (lax.rem(t + d, leaves), s),
            ).start()

    for k in units:
        wait_vw(0, k)
    send_root_weights(0)
    for j in range(early, per):
        take_halo(j)
    near_halo(early, per * chips)

    def far_halo(p):
        def step(k, carry):
            far_block(p, 1, k, None)
            return carry

        lax.fori_loop(0, subs, step, 0)

    def far_units(p):
        for k in units:
            far_block(p, 0, k, upper(k))

    far_halo(0)
    reduce_halo(0)
    far_units(0)
    for q in range(quota):

        @pl.when(present(q))
        def _():
            arrived(root_in.at[q], root_send.at[0], root_recv.at[q])

        @pl.when(jnp.logical_not(present(q)))
        def _():
            root_in[q] = root_own[...]

        rows = jnp.concatenate(augmented(root_in[q], scale, True), axis=0).T.astype(BF16)
        kroot_ref[q] = jnp.exp2(jnp.dot(rows, rcol_ref[...], preferred_element_type=F32))

    root_out = top(0)
    reduce_units(0, root_out)
    near_own()
    far_block(0, 0, 0, None)
    applied = reduce_finish(0, root_out)
    first = [tree[j] - (applied[j] + RIDGE_SHIFT * tree[j]) / ritz_ref[0] for j in range(per)]

    weigh(1, first)
    spread(1, 0)
    clear()
    near_diagonal()
    for k in units:
        wait_vw(1, k)
        spread(1, k)
    wait_vw(1, halo)
    spread(1, halo)
    send_root_weights(1)
    near_halo(0, per * chips)
    far_halo(1)
    reduce_halo(1)
    for k in units:
        near_unit(k)
    far_units(1)
    root_out = top(1)
    reduce_units(1, root_out)
    near_own()
    far_block(1, 0, 0, None)
    applied = reduce_finish(1, root_out)
    square = jnp.zeros((1, leaf_size), F32)
    placed = jnp.zeros((rows_all, LANES), F32)
    for j in range(per):
        v0 = vw_ref[0, 0, j : j + 1, 0:leaf_size]
        v1 = vw_ref[1, 0, j : j + 1, 0:leaf_size]
        second = v1 - (applied[j] + RIDGE_SHIFT * v1) / ritz_ref[1]
        grown = v0 - second
        square = square + grown * grown
        in_row, in_lane = hot_rows(order_of(0, j))
        held = jnp.concatenate(split3(jnp.where(in_row, grown, 0.0)), axis=0)
        hot = jnp.where(in_lane, 1.0, 0.0).astype(BF16)
        spots = lax.dot_general(
            held.astype(BF16), hot, (((1,), (1,)), ((), ())), preferred_element_type=F32
        )
        placed = placed + (
            spots[0:rows_all] + spots[rows_all : 2 * rows_all] + spots[2 * rows_all : 3 * rows_all]
        )
    placed_ref[...] = placed.reshape(subs, rows_own, LANES)
    for k in units:
        start(
            placed_ref.at[sub_of(k)],
            fin_in.at[inverse(k) - 1],
            fin_sem.at[0, k - 1],
            fin_sem.at[1, inverse(k) - 1],
            (t, sub_of(k)),
        )

    part = jnp.zeros((basis_count, LANES), F32)
    for k in range(subs):
        if k:
            arrived(bas_in.at[k - 1], bas_sem.at[0, k - 1], bas_sem.at[1, k - 1])
        spots = placed_ref[sub_of(k)]
        for r in range(rows_own):
            lanes = slice(r * LANES, (r + 1) * LANES)
            piece = basis_ref[:, lanes] if k == 0 else bas_in[k - 1, :, lanes]
            part = part + piece * spots[r : r + 1]
    corner = jnp.logical_and(lane_small == 1 + basis_count, sub_small == 0)
    tot_own[...] = (
        gram_ref[...]
        + jnp.where(lane_small == 0, jnp.sum(part, axis=1, keepdims=True), 0.0)
        + jnp.where(corner, jnp.sum(square, axis=1, keepdims=True), 0.0)
    )
    send_units(tot_own, tot_in, tots_sem)
    for k in units:
        arrived(tot_in.at[k - 1], tots_sem.at[0, k - 1], tots_sem.at[1, k - 1])
    tot_all[0] = tot_own[...]
    for k in units:
        tot_all[k] = tot_in[k - 1]
    total = tot_all[sub_order(chip, core, 0, chips)]
    for i in range(1, subs):
        total = total + tot_all[sub_order(chip, core, i, chips)]
    tot_sub[t] = total
    for d in range(1, leaves):
        start(
            tot_sub.at[t],
            tot_sub.at[t],
            totl_sem.at[0, d - 1],
            totl_sem.at[1, d - 1],
            (lax.rem(t + d, leaves), s),
        )
    user = placed_ref[s]
    for k in units:
        arrived(fin_in.at[k - 1], fin_sem.at[0, k - 1], fin_sem.at[1, k - 1])
        user = user + fin_in[k - 1]
    for d in range(1, leaves):
        slot = tot_sub.at[lax.rem(t + leaves - d, leaves)]
        arrived(slot, totl_sem.at[0, d - 1], totl_sem.at[1, d - 1])
    total = tot_sub[0]
    for u in range(1, leaves):
        total = total + tot_sub[u]
    proj = total[:, 0:1]
    squares = jnp.sum(jnp.where(corner, total, 0.0), keepdims=True)
    proj_row = jnp.sum(jnp.where(lane_small == 1 + sub_small, proj, 0.0), axis=0, keepdims=True)
    gram_proj = jnp.sum(
        jnp.where(jnp.logical_and(lane_small >= 1, lane_small <= basis_count), total, 0.0) * proj_row,
        axis=1,
        keepdims=True,
    )
    length_sq = (
        squares
        - 2.0 * jnp.sum(proj * proj, axis=0, keepdims=True)
        + jnp.sum(proj * gram_proj, axis=0, keepdims=True)
    )
    norm = jnp.sqrt(length_sq + EPSILON)
    hess = jnp.sum(jnp.where(lane_small == sub_small, proj, 0.0), axis=0, keepdims=True)
    hess_ref[...] = hess + jnp.where(lane_small[0:1] == basis_count, norm, 0.0)
    for r in range(rows_own):
        span = jnp.sum(basis_ref[:, r * LANES : (r + 1) * LANES] * proj, axis=0, keepdims=True)
        orth_ref[r : r + 1] = user[r : r + 1] - span

    for c in started:
        c.wait_send()

    @pl.when(s == home)
    def _():
        there = (next_leaf, s)
        for d in range(1, leaves):
            q = lax.div(t, subs)
            copy(root_own, root_in.at[q], root_send.at[d - 1], root_recv.at[q], there).wait_send()
            for p in range(2):
                copy(
                    wroot_own.at[p], wroot_in.at[p, q], wroot_send.at[p, d - 1], wroot_recv.at[p, q], there
                ).wait_send()


def sub_order(chip, core, i, chips):
    return lax.rem(i // 2 + chips - chip, chips) * 2 + lax.rem(i % 2 + 2 - core, 2)


def shards(
    points,
    leaf_maps,
    root_maps,
    current,
    krylov_basis,
    ritz_roots,
    point_order,
    skeleton,
    root_skeleton,
    near_list,
    far_list,
):
    per, skel, leaf_size = leaf_maps.shape
    feat = points.shape[1]
    subs, leaves = lax.axis_size("sub"), lax.axis_size("leaf")
    near_count, far_count = near_list.shape[1], far_list.shape[1]
    basis_count = krylov_basis.shape[0]
    dims = (per, leaf_size, feat, skel, leaves, subs, near_count, far_count, basis_count)
    cols, rows_own = per * subs, per * leaf_size // LANES
    quota = -(-leaves // subs)
    wide = leaf_size + skel
    dma = pltpu.SemaphoreType.DMA
    scratch = [
        pltpu.VMEM((per * leaf_size, feat), F32),
        pltpu.VMEM((per, feat, leaf_size), F32),
        pltpu.VMEM((per, skel, leaf_size), F32),
        pltpu.VMEM((per, skel, leaf_size), F32),
        pltpu.VMEM((basis_count, rows_own * LANES), F32),
        pltpu.VMEM((subs + 1, per, feat, leaf_size), F32),
        pltpu.VMEM((per, leaf_size), F32),
        pltpu.VMEM((subs, per, leaf_size), F32),
        pltpu.VMEM((subs - 1, rows_own, LANES), F32),
        pltpu.VMEM((subs - 1, rows_own, LANES), jnp.int32),
        pltpu.VMEM((subs - 1, basis_count, rows_own * LANES), F32),
        pltpu.VMEM((cols, 4 * feat, leaf_size), BF16),
        pltpu.VMEM((2 * per, leaf_size, 4 * feat), BF16),
        pltpu.VMEM((subs, 4 * feat, per * skel), BF16),
        pltpu.VMEM((2, per * skel, 4 * feat), BF16),
        pltpu.VMEM((cols + per, 3 * cols, LANES), F32),
        pltpu.VMEM((cols + per, 3 * cols, LANES), F32),
        pltpu.VMEM((2, subs + 1, 2 * per, wide), F32),
        pltpu.VMEM((cols, 1, leaf_size), F32),
        pltpu.VMEM((2 * per, leaf_size, LANES), F32),
        pltpu.VMEM((2, per * skel, LANES), F32),
        pltpu.VMEM((cols, 8, leaf_size), F32),
        pltpu.VMEM((2 * per, leaf_size, LANES), F32),
        pltpu.VMEM((subs, 8, per * skel), F32),
        pltpu.VMEM((2, per * skel, LANES), F32),
        pltpu.VMEM((feat, skel), F32),
        pltpu.VMEM((quota, feat, skel), F32),
        pltpu.VMEM((4 * feat, skel), BF16),
        pltpu.VMEM((quota, skel, LANES), F32),
        pltpu.VMEM((2, 8, skel), F32),
        pltpu.VMEM((2, quota, 8, skel), F32),
        pltpu.VMEM((2, subs, 2 * per, wide), F32),
        pltpu.VMEM((2, subs, 2 * per, wide), F32),
        pltpu.VMEM((subs, rows_own, LANES), F32),
        pltpu.VMEM((subs - 1, rows_own, LANES), F32),
        pltpu.VMEM((basis_count, LANES), F32),
        pltpu.VMEM((subs - 1, basis_count, LANES), F32),
        pltpu.VMEM((leaves, basis_count, LANES), F32),
        pltpu.VMEM((subs, basis_count, LANES), F32),
        pltpu.VMEM((basis_count, LANES), F32),
        dma((4,)),
        dma((2, subs - 1)),
        dma((2, subs - 1)),
        dma((2, subs - 1)),
        dma((2, subs)),
        dma((subs + 1, per)),
        dma((subs + 1, per)),
        dma((2, 2, subs)),
        dma((2, 2, subs)),
        dma((leaves - 1,)),
        dma((quota,)),
        dma((2, leaves - 1)),
        dma((2, quota)),
        dma((2, subs - 1)),
        dma((2, subs - 1)),
        dma((2, leaves - 1)),
    ]
    orth, hess = pl.pallas_call(
        lambda *refs: kernel_body(dims, *refs),
        out_shape=[
            jax.ShapeDtypeStruct((rows_own, LANES), F32),
            jax.ShapeDtypeStruct((1, LANES), F32),
        ],
        in_specs=[ANY] * 3 + [VMEM] * 6 + [ANY, SMEM],
        out_specs=[VMEM] * 2,
        scratch_shapes=scratch,
        compiler_params=pltpu.CompilerParams(
            collective_id=0, has_side_effects=True, vmem_limit_bytes=48 * 1024 * 1024
        ),
        name="step",
    )(
        points,
        leaf_maps,
        root_maps,
        current.reshape(rows_own, LANES),
        point_order.reshape(rows_own, LANES),
        skeleton,
        root_skeleton,
        near_list,
        far_list,
        krylov_basis,
        ritz_roots,
    )
    return orth.reshape(-1), hess[0, : basis_count + 1]


def solution(mesh):
    return jax.shard_map(
        shards,
        mesh=mesh,
        in_specs=(
            P(("leaf", "sub"), None),
            P(("leaf", "sub"), None, None),
            P(("leaf", "sub"), None, None),
            P(("leaf", "sub")),
            P(None, ("leaf", "sub")),
            P(),
            P(("leaf", "sub")),
            P(("leaf", "sub"), None),
            P("leaf", None),
            P(("leaf", "sub"), None),
            P(("leaf", "sub"), None),
        ),
        out_specs=(P(("leaf", "sub")), P()),
        check_vma=False,
    )
```

```python
import jax
import jax.numpy as jnp
from jax import lax
from jax.experimental import pallas as pl
from jax.experimental.pallas import tpu as pltpu
from jax.sharding import PartitionSpec as P

RIDGE_SHIFT = 1.0
EPSILON = 1e-06
LOG2E = 1.4426950408889634
LANES = 128
CHUNK = 512
MESH = pl.DeviceIdType.MESH
VMEM = pl.BlockSpec(memory_space=pltpu.VMEM)
ANY = pl.BlockSpec(memory_space=pl.ANY)
SMEM = pl.BlockSpec(memory_space=pltpu.SMEM)
F32, BF16 = jnp.float32, jnp.bfloat16


def bf16_part(x):
    return x.astype(BF16).astype(F32)


def augmented(x, scale, target):
    feat, size = x.shape
    sq = -scale * jnp.sum(x * x, axis=0, keepdims=True)
    s1 = bf16_part(sq)
    s2 = bf16_part(sq - s1)
    s3 = sq - s1 - s2
    row = lax.broadcasted_iota(jnp.int32, (feat, size), 0)
    first = 3 if target else 0
    ones = jnp.where(row < 6, 1.0, 0.0)
    extra = jnp.where(
        row == first,
        s1,
        jnp.where(row == first + 1, s2, jnp.where(row == first + 2, s3, ones)),
    )
    if target:
        x = x * (2.0 * scale)
    hi = bf16_part(x)
    lo = x - hi
    return (hi, lo, hi, extra) if target else (hi, hi, lo, extra)


def split3(x):
    hi = bf16_part(x)
    mid = bf16_part(x - hi)
    return hi, mid, x - hi - mid


def column_of(row):
    return jnp.broadcast_to(row, (LANES, row.shape[1])).T


def fold(block):
    return jnp.sum(block.reshape(block.shape[0] // 8, 8, LANES), axis=0)


def row_of(block):
    return jnp.sum(block.T, axis=0, keepdims=True)


def kernel_body(dims, *refs):
    (per, leaf_size, feat, skel, leaves, subs, near_count, far_count, basis_count) = dims
    (
        points_any,
        lmap_any,
        rmap_any,
        cur_ref,
        order_ref,
        skel_ref,
        rskel_ref,
        near_ref,
        far_ref,
        basis_any,
        ritz_ref,
        orth_ref,
        hess_ref,
        raw_ref,
        xt_ref,
        lmap_ref,
        rmap_ref,
        basis_ref,
        xin_ref,
        meta_own,
        meta_in,
        cur_in,
        ord_in,
        bas_in,
        col_ref,
        row_ref,
        zcol_ref,
        zrow_ref,
        ntab_ref,
        ftab_ref,
        vw_ref,
        vrow_ref,
        vb_ref,
        wb_ref,
        acc1_ref,
        acc2_ref,
        fac1_ref,
        fac2_ref,
        root_own,
        root_in,
        rcol_ref,
        kroot_ref,
        wroot_own,
        wroot_in,
        rs_out,
        rs_in,
        placed_ref,
        fin_in,
        tot_own,
        tot_in,
        tot_sub,
        tot_all,
        gram_ref,
        load_sem,
        cur_sem,
        ord_sem,
        bas_sem,
        meta_sem,
        pts_send,
        pts_recv,
        vw_sem,
        rs_sem,
        root_send,
        root_recv,
        wroot_send,
        wroot_recv,
        fin_sem,
        tots_sem,
        totl_sem,
    ) = refs
    t, s = lax.axis_index("leaf"), lax.axis_index("sub")
    chips = subs // 2
    chip, core = lax.div(s, 2), lax.rem(s, 2)
    cols = per * subs
    groups = leaf_size // LANES
    rows_own = per * leaf_size // LANES
    rows_all = subs * rows_own
    scale = LOG2E / feat
    halo = subs
    quota = -(-leaves // subs)
    next_leaf, prev_leaf = lax.rem(t + 1, leaves), lax.rem(t + leaves - 1, leaves)
    units = range(1, subs)

    def sub_of(k):
        return lax.rem(chip + k // 2, chips) * 2 + lax.rem(core + k % 2, 2)

    def sub_of_dynamic(k):
        return lax.rem(chip + lax.div(k, 2), chips) * 2 + lax.rem(core + lax.rem(k, 2), 2)

    def inverse(k):
        return (chips - k // 2) % chips * 2 + k % 2

    def upper(k):
        return lax.div(s - sub_of(k) + subs - 1, subs)

    def copy(src, dst, send, recv, there):
        return pltpu.make_async_remote_copy(
            src_ref=src, dst_ref=dst, send_sem=send, recv_sem=recv, device_id=there, device_id_type=MESH
        )

    started = []

    def start(*args):
        c = copy(*args)
        c.start()
        started.append(c)

    def arrived(dst, send, recv):
        copy(dst, dst, send, recv, (t, sub_of(1))).wait_recv()

    barrier = pltpu.get_barrier_semaphore()
    peers = [(lax.rem(t + d, leaves), s) for d in range(1, leaves)]
    peers += [(t, sub_of(k)) for k in units]
    for there in peers:
        pl.semaphore_signal(barrier, inc=1, device_id=there, device_id_type=MESH)

    loads = [
        pltpu.make_async_copy(src, dst, load_sem.at[i])
        for i, (src, dst) in enumerate(
            (
                (points_any, raw_ref),
                (basis_any, basis_ref),
                (lmap_any, lmap_ref),
                (rmap_any, rmap_ref),
            )
        )
    ]
    for c in loads:
        c.start()

    meta_own[...] = jnp.zeros_like(meta_own)
    meta_own[:, 0:skel] = skel_ref[...].astype(F32)
    meta_own[:, LANES : LANES + near_count] = near_ref[...].astype(F32)
    meta_own[:, 2 * LANES : 2 * LANES + far_count] = far_ref[...].astype(F32)
    def build_col(c, x):
        for i, piece in enumerate(augmented(x, scale, False)):
            col_ref[c, i * feat : (i + 1) * feat] = piece.astype(BF16)

    def build_row(r, x):
        pieces = augmented(x, scale, True)
        row_ref[r] = jnp.concatenate(pieces, axis=0).T.astype(BF16)

    def one_hot(index_row):
        spot = lax.broadcasted_iota(jnp.int32, (leaf_size, skel), 0)
        return jnp.where(spot == index_row, 1.0, 0.0)

    def meta_row(k, j, lane, count):
        if k == 0:
            return meta_own[j : j + 1, lane : lane + count]
        return meta_in[k - 1, j : j + 1, lane : lane + count]

    def build_tables(k, j):
        place = k * per + j
        slots = lax.broadcasted_iota(jnp.int32, (3 * cols, 1), 0).astype(F32)
        for table, lane, count in ((ntab_ref, LANES, near_count), (ftab_ref, 2 * LANES, far_count)):
            hit = jnp.where(slots == meta_row(k, j, lane, count), 1.0, 0.0)
            table[place] = jnp.broadcast_to(jnp.max(hit, axis=1, keepdims=True), (3 * cols, LANES))

    def build_skeleton(k, j, as_col, r):
        chosen = one_hot(meta_row(k, j, 0, skel).astype(jnp.int32))
        if as_col:
            picked = jnp.dot(col_ref[k * per + j], chosen.astype(BF16), preferred_element_type=F32)
            zcol_ref[k, :, j * skel : (j + 1) * skel] = picked.astype(BF16)
        if r is not None:
            picked = jnp.dot(chosen.T.astype(BF16), row_ref[r], preferred_element_type=F32)
            zrow_ref[r // per, j * skel : (j + 1) * skel, :] = picked.astype(BF16)

    loads[0].wait()
    for j in range(per):
        xt_ref[j] = raw_ref[j * leaf_size : (j + 1) * leaf_size, :].T
        build_col(j, xt_ref[j])
        build_row(j, xt_ref[j])
    for j in range(per):
        build_tables(0, j)
        build_skeleton(0, j, True, j)
    loads[1].wait()
    gram = jnp.zeros((basis_count, LANES), F32)
    lane_small = lax.broadcasted_iota(jnp.int32, (basis_count, LANES), 1)
    sub_small = lax.broadcasted_iota(jnp.int32, (basis_count, LANES), 0)
    for i in range(basis_count):
        total = jnp.zeros((basis_count, LANES), F32)
        for r in range(rows_own):
            piece = basis_ref[:, r * LANES : (r + 1) * LANES]
            total = total + piece * piece[i : i + 1]
        gram = gram + jnp.where(lane_small == 1 + i, jnp.sum(total, axis=1, keepdims=True), 0.0)
    gram_ref[...] = gram

    pl.semaphore_wait(barrier, len(peers))
    def send_units(src, dst, sem):
        for k in units:
            start(src, dst.at[inverse(k) - 1], sem.at[0, k - 1], sem.at[1, inverse(k) - 1], (t, sub_of(k)))

    across = [k for k in units if k % 2 == 0]
    sibling = 1

    def send_points(j):
        to = [(k, inverse(k), (t, sub_of(k))) for k in across]
        to += [(halo, halo, (prev_leaf, s)), (sibling, sibling, (t, sub_of(sibling)))]
        for k, slot, there in to:
            start(xt_ref.at[j], xin_ref.at[slot, j], pts_send.at[k, j], pts_recv.at[slot, j], there)

    early = per // 2
    send_units(cur_ref, cur_in, cur_sem)
    send_units(order_ref, ord_in, ord_sem)
    send_units(meta_own, meta_in, meta_sem)
    start(meta_own, meta_in.at[halo - 1], meta_sem.at[0, halo - 1], meta_sem.at[1, halo - 1], (prev_leaf, s))
    for j in range(early):
        send_points(j)

    for k in units:
        arrived(cur_in.at[k - 1], cur_sem.at[0, k - 1], cur_sem.at[1, k - 1])
    row_spot = lax.broadcasted_iota(jnp.int32, (rows_all, leaf_size), 0)
    lane_spot = lax.broadcasted_iota(jnp.int32, (LANES, leaf_size), 0)
    depth = -(-3 * rows_all // LANES) * LANES
    placed_ref[s] = cur_ref[...]
    for k in units:
        placed_ref[sub_of(k)] = cur_in[k - 1]
    pieces = split3(placed_ref[...].reshape(rows_all, LANES))
    pad = [jnp.zeros((depth - 3 * rows_all, LANES), F32)] if depth > 3 * rows_all else []
    stack = jnp.concatenate(list(pieces) + pad, axis=0).T.astype(BF16)

    def hot_rows(order):
        index = jnp.concatenate(order, axis=1)
        return (
            row_spot == lax.shift_right_logical(index, 7),
            lane_spot == lax.bitwise_and(index, LANES - 1),
        )

    def order_of(k, j):
        rows = range(j * groups, (j + 1) * groups)
        if k == 0:
            return [order_ref[r : r + 1, :] for r in rows]
        return [ord_in[k - 1, r : r + 1, :] for r in rows]

    def in_tree_order(k, j):
        in_row, in_lane = hot_rows(order_of(k, j))
        hot = jnp.where(in_row, 1.0, 0.0)
        fill = [jnp.zeros((depth - 3 * rows_all, leaf_size), F32)] if depth > 3 * rows_all else []
        picked = jnp.dot(
            stack, jnp.concatenate([hot] * 3 + fill, axis=0).astype(BF16), preferred_element_type=F32
        )
        return jnp.sum(jnp.where(in_lane, picked, 0.0), axis=0, keepdims=True)

    tree = [in_tree_order(0, j) for j in range(per)]

    def weigh(p, vectors):
        total = jnp.zeros((skel, LANES), F32)
        for j in range(per):
            part = jnp.zeros((skel, LANES), F32)
            for g in range(groups):
                piece = vectors[j][:, g * LANES : (g + 1) * LANES]
                part = part + lmap_ref[j, :, g * LANES : (g + 1) * LANES] * piece
                total = total + rmap_ref[j, :, g * LANES : (g + 1) * LANES] * piece
            vw_ref[p, 0, j : j + 1, 0:leaf_size] = vectors[j]
            vw_ref[p, 0, j : j + 1, leaf_size : leaf_size + skel] = row_of(part)
        vw_ref[p, 0, per : per + 1, 0:skel] = row_of(total)
        for k in units:
            start(
                vw_ref.at[p, 0],
                vw_ref.at[p, inverse(k)],
                vw_sem.at[p, 0, k - 1],
                vw_sem.at[p, 1, inverse(k) - 1],
                (t, sub_of(k)),
            )
        start(
            vw_ref.at[p, 0],
            vw_ref.at[p, halo],
            vw_sem.at[p, 0, halo - 1],
            vw_sem.at[p, 1, halo - 1],
            (prev_leaf, s),
        )

    def near_block(r, c, m1, m2):
        va = None
        if m2 is not None:
            va = [
                vrow_ref[c, :, g * LANES : (g + 1) * LANES] * m2
                for g in range(groups)
            ]
        acc = [jnp.zeros((8, LANES), F32) for _ in range(groups)]
        for m in range(0, leaf_size, CHUNK):
            inner = jnp.dot(row_ref[r, m : m + CHUNK], col_ref[c], preferred_element_type=F32)
            e = jnp.exp2(inner)
            w = vb_ref[r, m : m + CHUNK]
            tot = None
            for g in range(groups):
                piece = e[:, g * LANES : (g + 1) * LANES]
                acc[g] = acc[g] + fold(piece * w)
                if va is not None:
                    q = piece * va[g]
                    tot = q if tot is None else tot + q
            if va is not None:
                acc2_ref[r, m : m + CHUNK] += tot
        for g in range(groups):
            acc1_ref[c, :, g * LANES : (g + 1) * LANES] += acc[g] * m1

    def table_row(table, place, slot):
        return table[place, pl.ds(slot, 1), :]

    def own_pair(r, c, k, j, both=True):
        m1 = table_row(ntab_ref, c, cols + s * per + r)
        m2 = table_row(ntab_ref, r, cols + sub_of(k) * per + j) if both else None
        near_block(r, c, m1, m2)

    def near_diagonal():
        def diagonal(i, carry):
            own_pair(i, i, 0, i, False)
            return carry

        lax.fori_loop(0, per, diagonal, 0, unroll=per)

    def near_own():
        for d in range(1, per // 2 + 1):
            count = per if 2 * d < per else per // 2

            def pair(i, carry):
                j = lax.rem(i + d, per)
                own_pair(i, j, 0, j)
                return carry

            lax.fori_loop(0, count, pair, 0, unroll=count)

    def near_unit(k):
        half = per // 2

        def pair(b, carry):
            o = lax.div(b, half)
            j = 2 * lax.rem(b, half) + lax.rem(o + upper(k), 2)
            own_pair(o, k * per + j, k, j)
            return carry

        lax.fori_loop(0, per * half, pair, 0, unroll=per * half)

    def near_halo(first, last):
        def outer(run, carry):
            i, pair = lax.rem(run, per), lax.div(run, per)

            def step(b, carry):
                c = pair * 2 * per + b
                place = sub_of_dynamic(lax.div(c, per)) * per + lax.rem(c, per)
                m1 = table_row(ntab_ref, c, 2 * cols + s * per + i)
                m2 = table_row(ntab_ref, cols + i, place)
                near_block(per + i, c, m1, m2)
                return carry

            return lax.fori_loop(0, 2 * per, step, carry, unroll=2 * per)

        lax.fori_loop(first, last, outer, 0)

    def far_block(p, r, k, parity):
        inner = jnp.dot(zrow_ref[r], zcol_ref[k], preferred_element_type=F32)
        both = parity is not None or r == 1
        for i in range(per):
            acc, ways = [], []
            for j in range(per):
                peer = sub_of(k) * per + j
                slot = (cols if r == 0 else 2 * cols) + s * per + i
                m1 = table_row(ftab_ref, k * per + j, slot)
                m2 = table_row(ftab_ref, i if r == 0 else cols + i, (cols if r == 0 else 0) + peer)
                if parity is not None:
                    use = (1 - lax.rem(parity + i + j, 2)).astype(F32)
                    m1, m2 = m1 * use, m2 * use
                w = vw_ref[p, k, j : j + 1, leaf_size : leaf_size + skel]
                ways.append((m1, w * m2))
            rows = slice(i * skel, (i + 1) * skel)
            e = jnp.exp2(inner[rows])
            wb = wb_ref[r, rows]
            tot = None
            for j in range(per):
                piece = e[:, j * skel : (j + 1) * skel]
                acc.append(fold(piece * wb))
                if both:
                    q = piece * ways[j][1]
                    tot = q if tot is None else tot + q
            if both:
                fac2_ref[r, rows] += tot
            for j in range(per):
                fac1_ref[k, :, j * skel : (j + 1) * skel] += acc[j] * ways[j][0]

    def spread(p, k):
        for j in range(per):
            value = vw_ref[p, k, j : j + 1, 0:leaf_size]
            if k != halo:
                vrow_ref[k * per + j] = value
            if k in (0, halo):
                r = j if k == 0 else per + j
                vb_ref[r] = column_of(value)
                wb_ref[r // per, j * skel : (j + 1) * skel] = column_of(
                    vw_ref[p, k, j : j + 1, leaf_size : leaf_size + skel]
                )

    def wait_vw(p, k):
        arrived(vw_ref.at[p, k], vw_sem.at[p, 0, k - 1], vw_sem.at[p, 1, k - 1])

    def clear():
        acc1_ref[...] = jnp.zeros_like(acc1_ref)
        acc2_ref[...] = jnp.zeros_like(acc2_ref)
        fac1_ref[...] = jnp.zeros_like(fac1_ref)
        fac2_ref[...] = jnp.zeros_like(fac2_ref)

    home = lax.rem(t, subs)

    def send_root_weights(p):
        total = vw_ref[p, 0, per : per + 1, 0:skel]
        for k in units:
            total = total + vw_ref[p, k, per : per + 1, 0:skel]
        wroot_own[p] = jnp.broadcast_to(total, (8, skel))

        @pl.when(s == home)
        def _():
            for d in range(1, leaves):
                copy(
                    wroot_own.at[p],
                    wroot_in.at[p, lax.div(t, subs)],
                    wroot_send.at[p, d - 1],
                    wroot_recv.at[p, lax.div(t, subs)],
                    (lax.rem(t + d, leaves), s),
                ).start()

    def root_of(q):
        return q * subs + s

    def present(q):
        u = root_of(q)
        return jnp.logical_and(u != t, u < leaves)

    def top(p):
        total = jnp.zeros((8, LANES), F32)
        for q in range(quota):

            @pl.when(present(q))
            def _():
                arrived(wroot_in.at[p, q], wroot_send.at[p, 0], wroot_recv.at[p, q])

            @pl.when(jnp.logical_not(present(q)))
            def _():
                wroot_in[p, q] = jnp.zeros((8, skel), F32)

            column = column_of(wroot_in[p, q, 0:1, :])
            total = total + fold(kroot_ref[q] * column)
        return jnp.sum(total, axis=0, keepdims=True)

    def reduce_halo(p):
        for j in range(per):
            rs_out[p, 0, j : j + 1, 0:leaf_size] = row_of(acc2_ref[per + j])
            rs_out[p, 0, j : j + 1, leaf_size : leaf_size + skel] = row_of(
                fac2_ref[1, j * skel : (j + 1) * skel]
            )
        start(
            rs_out.at[p, 0],
            rs_in.at[p, halo - 1],
            rs_sem.at[p, 0, halo - 1],
            rs_sem.at[p, 1, halo - 1],
            (next_leaf, s),
        )

    def reduce_units(p, root_out):
        for k in units:
            for j in range(per):
                c = k * per + j
                rs_out[p, k, j : j + 1, 0:leaf_size] = jnp.sum(acc1_ref[c], axis=0, keepdims=True)
            rs_out[p, k, 0:per, leaf_size : leaf_size + skel] = jnp.concatenate(
                [
                    jnp.sum(fac1_ref[k, :, j * skel : (j + 1) * skel], axis=0, keepdims=True)
                    for j in range(per)
                ],
                axis=0,
            )
            rs_out[p, k, per : per + 1, 0:skel] = root_out
            start(
                rs_out.at[p, k],
                rs_in.at[p, inverse(k) - 1],
                rs_sem.at[p, 0, k - 1],
                rs_sem.at[p, 1, inverse(k) - 1],
                (t, sub_of(k)),
            )

    def reduce_finish(p, root_out):
        nears, fars = [], []
        for j in range(per):
            nears.append(jnp.sum(acc1_ref[j], axis=0, keepdims=True) + row_of(acc2_ref[j]))
            fars.append(
                jnp.sum(fac1_ref[0, :, j * skel : (j + 1) * skel], axis=0, keepdims=True)
                + row_of(fac2_ref[0, j * skel : (j + 1) * skel])
            )
        for k in range(1, subs + 1):
            arrived(rs_in.at[p, k - 1], rs_sem.at[p, 0, k - 1], rs_sem.at[p, 1, k - 1])
            for j in range(per):
                nears[j] = nears[j] + rs_in[p, k - 1, j : j + 1, 0:leaf_size]
                fars[j] = fars[j] + rs_in[p, k - 1, j : j + 1, leaf_size : leaf_size + skel]
            if k < subs:
                root_out = root_out + rs_in[p, k - 1, per : per + 1, 0:skel]
        root_column = column_of(root_out)
        applied = []
        for j in range(per):
            far_column = column_of(fars[j])
            parts = []
            for g in range(groups):
                lanes = slice(g * LANES, (g + 1) * LANES)
                both = lmap_ref[j, :, lanes] * far_column + rmap_ref[j, :, lanes] * root_column
                parts.append(jnp.sum(both, axis=0, keepdims=True))
            applied.append(nears[j] + jnp.concatenate(parts, axis=1))
        return applied

    loads[2].wait()
    loads[3].wait()
    weigh(0, tree)
    for j in range(early, per):
        send_points(j)
    send_units(basis_ref, bas_in, bas_sem)
    spread(0, 0)
    for k in units:
        arrived(ord_in.at[k - 1], ord_sem.at[0, k - 1], ord_sem.at[1, k - 1])
        for j in range(per):
            vrow_ref[k * per + j] = in_tree_order(k, j)
    clear()
    near_diagonal()

    def forward(j):
        for k in across:
            arrived(xin_ref.at[k, j], pts_send.at[k, j], pts_recv.at[k, j])
            start(
                xin_ref.at[k, j],
                xin_ref.at[k + 1, j],
                pts_send.at[k + 1, j],
                pts_recv.at[k + 1, j],
                (t, sub_of(sibling)),
            )

    def take_points(k):
        arrived(meta_in.at[k - 1], meta_sem.at[0, k - 1], meta_sem.at[1, k - 1])
        for j in range(per):
            if k not in across:
                arrived(xin_ref.at[k, j], pts_send.at[k, j], pts_recv.at[k, j])
        for j in range(per):
            build_col(k * per + j, xin_ref[k, j])
            build_tables(k, j)
            build_skeleton(k, j, True, None)

    def take_halo(j):
        arrived(xin_ref.at[halo, j], pts_send.at[halo, j], pts_recv.at[halo, j])
        build_row(per + j, xin_ref[halo, j])
        build_tables(halo, j)
        build_skeleton(halo, j, False, per + j)

    forward(0)
    take_points(sibling)
    near_unit(sibling)
    for j in range(1, early):
        forward(j)
    arrived(meta_in.at[halo - 1], meta_sem.at[0, halo - 1], meta_sem.at[1, halo - 1])
    wait_vw(0, halo)
    spread(0, halo)
    for j in range(early):
        take_halo(j)
    near_halo(0, early)
    for j in range(early, per):
        forward(j)
    for k in units:
        if k != sibling:
            take_points(k)
            near_unit(k)

    root_points = jnp.zeros((4 * feat, skel), F32)
    for k in range(subs):
        for j in range(per):
            base = (sub_of(k) * per + j) * leaf_size
            chosen = one_hot(rskel_ref[...] - base)
            root_points = root_points + jnp.dot(
                col_ref[k * per + j], chosen.astype(BF16), preferred_element_type=F32
            )
    rcol_ref[...] = root_points.astype(BF16)
    root_own[...] = root_points[0:feat] + root_points[2 * feat : 3 * feat]

    @pl.when(s == home)
    def _():
        for d in range(1, leaves):
            copy(
                root_own,
                root_in.at[lax.div(t, subs)],
                root_send.at[d - 1],
                root_recv.at[lax.div(t, subs)],
                (lax.rem(t + d, leaves), s),
            ).start()

    for k in units:
        wait_vw(0, k)
    send_root_weights(0)
    for j in range(early, per):
        take_halo(j)
    near_halo(early, per * chips)

    def far_halo(p):
        for k in range(subs):
            far_block(p, 1, k, None)

    def far_units(p):
        for k in units:
            far_block(p, 0, k, upper(k))

    far_halo(0)
    reduce_halo(0)
    far_units(0)
    for q in range(quota):

        @pl.when(present(q))
        def _():
            arrived(root_in.at[q], root_send.at[0], root_recv.at[q])

        @pl.when(jnp.logical_not(present(q)))
        def _():
            root_in[q] = root_own[...]

        rows = jnp.concatenate(augmented(root_in[q], scale, True), axis=0).T.astype(BF16)
        kroot_ref[q] = jnp.exp2(jnp.dot(rows, rcol_ref[...], preferred_element_type=F32))

    root_out = top(0)
    reduce_units(0, root_out)
    near_own()
    far_block(0, 0, 0, None)
    applied = reduce_finish(0, root_out)
    first = [tree[j] - (applied[j] + RIDGE_SHIFT * tree[j]) / ritz_ref[0] for j in range(per)]

    weigh(1, first)
    spread(1, 0)
    clear()
    near_diagonal()
    for k in units:
        wait_vw(1, k)
        spread(1, k)
    wait_vw(1, halo)
    spread(1, halo)
    send_root_weights(1)
    near_halo(0, per * chips)
    far_halo(1)
    reduce_halo(1)
    for k in units:
        near_unit(k)
    far_units(1)
    root_out = top(1)
    reduce_units(1, root_out)
    near_own()
    far_block(1, 0, 0, None)
    applied = reduce_finish(1, root_out)
    square = jnp.zeros((1, leaf_size), F32)
    placed = jnp.zeros((rows_all, LANES), F32)
    for j in range(per):
        v0 = vw_ref[0, 0, j : j + 1, 0:leaf_size]
        v1 = vw_ref[1, 0, j : j + 1, 0:leaf_size]
        second = v1 - (applied[j] + RIDGE_SHIFT * v1) / ritz_ref[1]
        grown = v0 - second
        square = square + grown * grown
        in_row, in_lane = hot_rows(order_of(0, j))
        held = jnp.concatenate(split3(jnp.where(in_row, grown, 0.0)), axis=0)
        hot = jnp.where(in_lane, 1.0, 0.0).astype(BF16)
        spots = lax.dot_general(
            held.astype(BF16), hot, (((1,), (1,)), ((), ())), preferred_element_type=F32
        )
        placed = placed + (
            spots[0:rows_all] + spots[rows_all : 2 * rows_all] + spots[2 * rows_all : 3 * rows_all]
        )
    placed_ref[...] = placed.reshape(subs, rows_own, LANES)
    for k in units:
        start(
            placed_ref.at[sub_of(k)],
            fin_in.at[inverse(k) - 1],
            fin_sem.at[0, k - 1],
            fin_sem.at[1, inverse(k) - 1],
            (t, sub_of(k)),
        )

    part = jnp.zeros((basis_count, LANES), F32)
    for k in range(subs):
        if k:
            arrived(bas_in.at[k - 1], bas_sem.at[0, k - 1], bas_sem.at[1, k - 1])
        spots = placed_ref[sub_of(k)]
        for r in range(rows_own):
            lanes = slice(r * LANES, (r + 1) * LANES)
            piece = basis_ref[:, lanes] if k == 0 else bas_in[k - 1, :, lanes]
            part = part + piece * spots[r : r + 1]
    corner = jnp.logical_and(lane_small == 1 + basis_count, sub_small == 0)
    tot_own[...] = (
        gram_ref[...]
        + jnp.where(lane_small == 0, jnp.sum(part, axis=1, keepdims=True), 0.0)
        + jnp.where(corner, jnp.sum(square, axis=1, keepdims=True), 0.0)
    )
    send_units(tot_own, tot_in, tots_sem)
    for k in units:
        arrived(tot_in.at[k - 1], tots_sem.at[0, k - 1], tots_sem.at[1, k - 1])
    tot_all[0] = tot_own[...]
    for k in units:
        tot_all[k] = tot_in[k - 1]
    total = tot_all[sub_order(chip, core, 0, chips)]
    for i in range(1, subs):
        total = total + tot_all[sub_order(chip, core, i, chips)]
    tot_sub[t] = total
    for d in range(1, leaves):
        start(
            tot_sub.at[t],
            tot_sub.at[t],
            totl_sem.at[0, d - 1],
            totl_sem.at[1, d - 1],
            (lax.rem(t + d, leaves), s),
        )
    user = placed_ref[s]
    for k in units:
        arrived(fin_in.at[k - 1], fin_sem.at[0, k - 1], fin_sem.at[1, k - 1])
        user = user + fin_in[k - 1]
    for d in range(1, leaves):
        slot = tot_sub.at[lax.rem(t + leaves - d, leaves)]
        arrived(slot, totl_sem.at[0, d - 1], totl_sem.at[1, d - 1])
    total = tot_sub[0]
    for u in range(1, leaves):
        total = total + tot_sub[u]
    proj = total[:, 0:1]
    squares = jnp.sum(jnp.where(corner, total, 0.0), keepdims=True)
    proj_row = jnp.sum(jnp.where(lane_small == 1 + sub_small, proj, 0.0), axis=0, keepdims=True)
    gram_proj = jnp.sum(
        jnp.where(jnp.logical_and(lane_small >= 1, lane_small <= basis_count), total, 0.0) * proj_row,
        axis=1,
        keepdims=True,
    )
    length_sq = (
        squares
        - 2.0 * jnp.sum(proj * proj, axis=0, keepdims=True)
        + jnp.sum(proj * gram_proj, axis=0, keepdims=True)
    )
    norm = jnp.sqrt(length_sq + EPSILON)
    hess = jnp.sum(jnp.where(lane_small == sub_small, proj, 0.0), axis=0, keepdims=True)
    hess_ref[...] = hess + jnp.where(lane_small[0:1] == basis_count, norm, 0.0)
    for r in range(rows_own):
        span = jnp.sum(basis_ref[:, r * LANES : (r + 1) * LANES] * proj, axis=0, keepdims=True)
        orth_ref[r : r + 1] = user[r : r + 1] - span

    for c in started:
        c.wait_send()

    @pl.when(s == home)
    def _():
        there = (next_leaf, s)
        for d in range(1, leaves):
            q = lax.div(t, subs)
            copy(root_own, root_in.at[q], root_send.at[d - 1], root_recv.at[q], there).wait_send()
            for p in range(2):
                copy(
                    wroot_own.at[p], wroot_in.at[p, q], wroot_send.at[p, d - 1], wroot_recv.at[p, q], there
                ).wait_send()


def sub_order(chip, core, i, chips):
    return lax.rem(i // 2 + chips - chip, chips) * 2 + lax.rem(i % 2 + 2 - core, 2)


def shards(
    points,
    leaf_maps,
    root_maps,
    current,
    krylov_basis,
    ritz_roots,
    point_order,
    skeleton,
    root_skeleton,
    near_list,
    far_list,
):
    per, skel, leaf_size = leaf_maps.shape
    feat = points.shape[1]
    subs, leaves = lax.axis_size("sub"), lax.axis_size("leaf")
    near_count, far_count = near_list.shape[1], far_list.shape[1]
    basis_count = krylov_basis.shape[0]
    dims = (per, leaf_size, feat, skel, leaves, subs, near_count, far_count, basis_count)
    cols, rows_own = per * subs, per * leaf_size // LANES
    quota = -(-leaves // subs)
    wide = leaf_size + skel
    dma = pltpu.SemaphoreType.DMA
    scratch = [
        pltpu.VMEM((per * leaf_size, feat), F32),
        pltpu.VMEM((per, feat, leaf_size), F32),
        pltpu.VMEM((per, skel, leaf_size), F32),
        pltpu.VMEM((per, skel, leaf_size), F32),
        pltpu.VMEM((basis_count, rows_own * LANES), F32),
        pltpu.VMEM((subs + 1, per, feat, leaf_size), F32),
        pltpu.VMEM((per, leaf_size), F32),
        pltpu.VMEM((subs, per, leaf_size), F32),
        pltpu.VMEM((subs - 1, rows_own, LANES), F32),
        pltpu.VMEM((subs - 1, rows_own, LANES), jnp.int32),
        pltpu.VMEM((subs - 1, basis_count, rows_own * LANES), F32),
        pltpu.VMEM((cols, 4 * feat, leaf_size), BF16),
        pltpu.VMEM((2 * per, leaf_size, 4 * feat), BF16),
        pltpu.VMEM((subs, 4 * feat, per * skel), BF16),
        pltpu.VMEM((2, per * skel, 4 * feat), BF16),
        pltpu.VMEM((cols + per, 3 * cols, LANES), F32),
        pltpu.VMEM((cols + per, 3 * cols, LANES), F32),
        pltpu.VMEM((2, subs + 1, 2 * per, wide), F32),
        pltpu.VMEM((cols, 1, leaf_size), F32),
        pltpu.VMEM((2 * per, leaf_size, LANES), F32),
        pltpu.VMEM((2, per * skel, LANES), F32),
        pltpu.VMEM((cols, 8, leaf_size), F32),
        pltpu.VMEM((2 * per, leaf_size, LANES), F32),
        pltpu.VMEM((subs, 8, per * skel), F32),
        pltpu.VMEM((2, per * skel, LANES), F32),
        pltpu.VMEM((feat, skel), F32),
        pltpu.VMEM((quota, feat, skel), F32),
        pltpu.VMEM((4 * feat, skel), BF16),
        pltpu.VMEM((quota, skel, LANES), F32),
        pltpu.VMEM((2, 8, skel), F32),
        pltpu.VMEM((2, quota, 8, skel), F32),
        pltpu.VMEM((2, subs, 2 * per, wide), F32),
        pltpu.VMEM((2, subs, 2 * per, wide), F32),
        pltpu.VMEM((subs, rows_own, LANES), F32),
        pltpu.VMEM((subs - 1, rows_own, LANES), F32),
        pltpu.VMEM((basis_count, LANES), F32),
        pltpu.VMEM((subs - 1, basis_count, LANES), F32),
        pltpu.VMEM((leaves, basis_count, LANES), F32),
        pltpu.VMEM((subs, basis_count, LANES), F32),
        pltpu.VMEM((basis_count, LANES), F32),
        dma((4,)),
        dma((2, subs - 1)),
        dma((2, subs - 1)),
        dma((2, subs - 1)),
        dma((2, subs)),
        dma((subs + 1, per)),
        dma((subs + 1, per)),
        dma((2, 2, subs)),
        dma((2, 2, subs)),
        dma((leaves - 1,)),
        dma((quota,)),
        dma((2, leaves - 1)),
        dma((2, quota)),
        dma((2, subs - 1)),
        dma((2, subs - 1)),
        dma((2, leaves - 1)),
    ]
    orth, hess = pl.pallas_call(
        lambda *refs: kernel_body(dims, *refs),
        out_shape=[
            jax.ShapeDtypeStruct((rows_own, LANES), F32),
            jax.ShapeDtypeStruct((1, LANES), F32),
        ],
        in_specs=[ANY] * 3 + [VMEM] * 6 + [ANY, SMEM],
        out_specs=[VMEM] * 2,
        scratch_shapes=scratch,
        compiler_params=pltpu.CompilerParams(
            collective_id=0, has_side_effects=True, vmem_limit_bytes=48 * 1024 * 1024
        ),
        name="step",
    )(
        points,
        leaf_maps,
        root_maps,
        current.reshape(rows_own, LANES),
        point_order.reshape(rows_own, LANES),
        skeleton,
        root_skeleton,
        near_list,
        far_list,
        krylov_basis,
        ritz_roots,
    )
    return orth.reshape(-1), hess[0, : basis_count + 1]


def solution(mesh):
    return jax.shard_map(
        shards,
        mesh=mesh,
        in_specs=(
            P(("leaf", "sub"), None),
            P(("leaf", "sub"), None, None),
            P(("leaf", "sub"), None, None),
            P(("leaf", "sub")),
            P(None, ("leaf", "sub")),
            P(),
            P(("leaf", "sub")),
            P(("leaf", "sub"), None),
            P("leaf", None),
            P(("leaf", "sub"), None),
            P(("leaf", "sub"), None),
        ),
        out_specs=(P(("leaf", "sub")), P()),
        check_vma=False,
    )
```

```python
import jax
import jax.numpy as jnp
from jax import lax
from jax.experimental import pallas as pl
from jax.experimental.pallas import tpu as pltpu
from jax.sharding import PartitionSpec as P

RIDGE_SHIFT = 1.0
EPSILON = 1e-06
LOG2E = 1.4426950408889634
LANES = 128
CHUNK = 512
MESH = pl.DeviceIdType.MESH
VMEM = pl.BlockSpec(memory_space=pltpu.VMEM)
ANY = pl.BlockSpec(memory_space=pl.ANY)
SMEM = pl.BlockSpec(memory_space=pltpu.SMEM)
F32, BF16 = jnp.float32, jnp.bfloat16


def bf16_part(x):
    return x.astype(BF16).astype(F32)


def augmented(x, scale, target):
    feat, size = x.shape
    sq = -scale * jnp.sum(x * x, axis=0, keepdims=True)
    s1 = bf16_part(sq)
    s2 = bf16_part(sq - s1)
    s3 = sq - s1 - s2
    row = lax.broadcasted_iota(jnp.int32, (feat, size), 0)
    first = 3 if target else 0
    ones = jnp.where(row < 6, 1.0, 0.0)
    extra = jnp.where(
        row == first,
        s1,
        jnp.where(row == first + 1, s2, jnp.where(row == first + 2, s3, ones)),
    )
    if target:
        x = x * (2.0 * scale)
    hi = bf16_part(x)
    lo = x - hi
    return (hi, lo, hi, extra) if target else (hi, hi, lo, extra)


def split3(x):
    hi = bf16_part(x)
    mid = bf16_part(x - hi)
    return hi, mid, x - hi - mid


def column_of(row):
    return jnp.broadcast_to(row, (LANES, row.shape[1])).T


def fold(block):
    return jnp.sum(block.reshape(block.shape[0] // 8, 8, LANES), axis=0)


def row_of(block):
    return jnp.sum(block.T, axis=0, keepdims=True)


def kernel_body(dims, *refs):
    (per, leaf_size, feat, skel, leaves, subs, near_count, far_count, basis_count) = dims
    (
        points_any,
        lmap_any,
        rmap_any,
        cur_ref,
        order_ref,
        skel_ref,
        rskel_ref,
        near_ref,
        far_ref,
        basis_any,
        ritz_ref,
        orth_ref,
        hess_ref,
        raw_ref,
        xt_ref,
        lmap_ref,
        rmap_ref,
        basis_ref,
        xin_ref,
        meta_own,
        meta_in,
        cur_in,
        ord_in,
        bas_in,
        col_ref,
        row_ref,
        zcol_ref,
        zrow_ref,
        ntab_ref,
        ftab_ref,
        vw_ref,
        vrow_ref,
        vb_ref,
        wb_ref,
        acc1_ref,
        acc2_ref,
        fac1_ref,
        fac2_ref,
        root_own,
        root_in,
        rcol_ref,
        kroot_ref,
        wroot_own,
        wroot_in,
        rs_out,
        rs_in,
        placed_ref,
        fin_in,
        tot_own,
        tot_in,
        tot_sub,
        tot_all,
        gram_ref,
        load_sem,
        cur_sem,
        ord_sem,
        bas_sem,
        meta_sem,
        pts_send,
        pts_recv,
        vw_sem,
        rs_sem,
        root_send,
        root_recv,
        wroot_send,
        wroot_recv,
        fin_sem,
        tots_sem,
        totl_sem,
    ) = refs
    t, s = lax.axis_index("leaf"), lax.axis_index("sub")
    chips = subs // 2
    chip, core = lax.div(s, 2), lax.rem(s, 2)
    cols = per * subs
    groups = leaf_size // LANES
    rows_own = per * leaf_size // LANES
    rows_all = subs * rows_own
    scale = LOG2E / feat
    halo = subs
    quota = -(-leaves // subs)
    next_leaf, prev_leaf = lax.rem(t + 1, leaves), lax.rem(t + leaves - 1, leaves)
    units = range(1, subs)

    def sub_of(k):
        return lax.rem(chip + k // 2, chips) * 2 + lax.rem(core + k % 2, 2)

    def sub_of_dynamic(k):
        return lax.rem(chip + lax.div(k, 2), chips) * 2 + lax.rem(core + lax.rem(k, 2), 2)

    def inverse(k):
        return (chips - k // 2) % chips * 2 + k % 2

    def upper(k):
        return lax.div(s - sub_of(k) + subs - 1, subs)

    def copy(src, dst, send, recv, there):
        return pltpu.make_async_remote_copy(
            src_ref=src, dst_ref=dst, send_sem=send, recv_sem=recv, device_id=there, device_id_type=MESH
        )

    started = []

    def start(*args):
        c = copy(*args)
        c.start()
        started.append(c)

    def arrived(dst, send, recv):
        copy(dst, dst, send, recv, (t, sub_of(1))).wait_recv()

    barrier = pltpu.get_barrier_semaphore()
    peers = [(lax.rem(t + d, leaves), s) for d in range(1, leaves)]
    peers += [(t, sub_of(k)) for k in units]
    for there in peers:
        pl.semaphore_signal(barrier, inc=1, device_id=there, device_id_type=MESH)

    loads = [
        pltpu.make_async_copy(src, dst, load_sem.at[i])
        for i, (src, dst) in enumerate(
            (
                (points_any, raw_ref),
                (basis_any, basis_ref),
                (lmap_any, lmap_ref),
                (rmap_any, rmap_ref),
            )
        )
    ]
    for c in loads:
        c.start()

    meta_own[...] = jnp.zeros_like(meta_own)
    meta_own[:, 0:skel] = skel_ref[...].astype(F32)
    meta_own[:, LANES : LANES + near_count] = near_ref[...].astype(F32)
    meta_own[:, 2 * LANES : 2 * LANES + far_count] = far_ref[...].astype(F32)
    def build_col(c, x):
        for i, piece in enumerate(augmented(x, scale, False)):
            col_ref[c, i * feat : (i + 1) * feat] = piece.astype(BF16)

    def build_row(r, x):
        pieces = augmented(x, scale, True)
        row_ref[r] = jnp.concatenate(pieces, axis=0).T.astype(BF16)

    def one_hot(index_row):
        spot = lax.broadcasted_iota(jnp.int32, (leaf_size, skel), 0)
        return jnp.where(spot == index_row, 1.0, 0.0)

    def meta_row(k, j, lane, count):
        if k == 0:
            return meta_own[j : j + 1, lane : lane + count]
        return meta_in[k - 1, j : j + 1, lane : lane + count]

    def build_tables(k, j):
        place = k * per + j
        slots = lax.broadcasted_iota(jnp.int32, (3 * cols, 1), 0).astype(F32)
        for table, lane, count in ((ntab_ref, LANES, near_count), (ftab_ref, 2 * LANES, far_count)):
            hit = jnp.where(slots == meta_row(k, j, lane, count), 1.0, 0.0)
            table[place] = jnp.broadcast_to(jnp.max(hit, axis=1, keepdims=True), (3 * cols, LANES))

    def build_skeleton(k, j, as_col, r):
        chosen = one_hot(meta_row(k, j, 0, skel).astype(jnp.int32))
        if as_col:
            picked = jnp.dot(col_ref[k * per + j], chosen.astype(BF16), preferred_element_type=F32)
            zcol_ref[k, :, j * skel : (j + 1) * skel] = picked.astype(BF16)
        if r is not None:
            picked = jnp.dot(chosen.T.astype(BF16), row_ref[r], preferred_element_type=F32)
            zrow_ref[r // per, j * skel : (j + 1) * skel, :] = picked.astype(BF16)

    loads[0].wait()
    for j in range(per):
        xt_ref[j] = raw_ref[j * leaf_size : (j + 1) * leaf_size, :].T
        build_col(j, xt_ref[j])
        build_row(j, xt_ref[j])
    for j in range(per):
        build_tables(0, j)
        build_skeleton(0, j, True, j)
    loads[1].wait()
    gram = jnp.zeros((basis_count, LANES), F32)
    lane_small = lax.broadcasted_iota(jnp.int32, (basis_count, LANES), 1)
    sub_small = lax.broadcasted_iota(jnp.int32, (basis_count, LANES), 0)
    for i in range(basis_count):
        total = jnp.zeros((basis_count, LANES), F32)
        for r in range(rows_own):
            piece = basis_ref[:, r * LANES : (r + 1) * LANES]
            total = total + piece * piece[i : i + 1]
        gram = gram + jnp.where(lane_small == 1 + i, jnp.sum(total, axis=1, keepdims=True), 0.0)
    gram_ref[...] = gram

    pl.semaphore_wait(barrier, len(peers))
    def send_units(src, dst, sem):
        for k in units:
            start(src, dst.at[inverse(k) - 1], sem.at[0, k - 1], sem.at[1, inverse(k) - 1], (t, sub_of(k)))

    across = [k for k in units if k % 2 == 0]
    sibling = 1

    def send_points(j):
        to = [(k, inverse(k), (t, sub_of(k))) for k in across]
        to += [(halo, halo, (prev_leaf, s)), (sibling, sibling, (t, sub_of(sibling)))]
        for k, slot, there in to:
            start(xt_ref.at[j], xin_ref.at[slot, j], pts_send.at[k, j], pts_recv.at[slot, j], there)

    early = per // 2
    send_units(cur_ref, cur_in, cur_sem)
    send_units(order_ref, ord_in, ord_sem)
    send_units(meta_own, meta_in, meta_sem)
    start(meta_own, meta_in.at[halo - 1], meta_sem.at[0, halo - 1], meta_sem.at[1, halo - 1], (prev_leaf, s))
    for j in range(early):
        send_points(j)

    for k in units:
        arrived(cur_in.at[k - 1], cur_sem.at[0, k - 1], cur_sem.at[1, k - 1])
    row_spot = lax.broadcasted_iota(jnp.int32, (rows_all, leaf_size), 0)
    lane_spot = lax.broadcasted_iota(jnp.int32, (LANES, leaf_size), 0)
    depth = -(-3 * rows_all // LANES) * LANES
    placed_ref[s] = cur_ref[...]
    for k in units:
        placed_ref[sub_of(k)] = cur_in[k - 1]
    pieces = split3(placed_ref[...].reshape(rows_all, LANES))
    pad = [jnp.zeros((depth - 3 * rows_all, LANES), F32)] if depth > 3 * rows_all else []
    stack = jnp.concatenate(list(pieces) + pad, axis=0).T.astype(BF16)

    def hot_rows(order):
        index = jnp.concatenate(order, axis=1)
        return (
            row_spot == lax.shift_right_logical(index, 7),
            lane_spot == lax.bitwise_and(index, LANES - 1),
        )

    def order_of(k, j):
        rows = range(j * groups, (j + 1) * groups)
        if k == 0:
            return [order_ref[r : r + 1, :] for r in rows]
        return [ord_in[k - 1, r : r + 1, :] for r in rows]

    def in_tree_order(k, j):
        in_row, in_lane = hot_rows(order_of(k, j))
        hot = jnp.where(in_row, 1.0, 0.0)
        fill = [jnp.zeros((depth - 3 * rows_all, leaf_size), F32)] if depth > 3 * rows_all else []
        picked = jnp.dot(
            stack, jnp.concatenate([hot] * 3 + fill, axis=0).astype(BF16), preferred_element_type=F32
        )
        return jnp.sum(jnp.where(in_lane, picked, 0.0), axis=0, keepdims=True)

    tree = [in_tree_order(0, j) for j in range(per)]

    def weigh(p, vectors):
        total = jnp.zeros((skel, LANES), F32)
        for j in range(per):
            part = jnp.zeros((skel, LANES), F32)
            for g in range(groups):
                piece = vectors[j][:, g * LANES : (g + 1) * LANES]
                part = part + lmap_ref[j, :, g * LANES : (g + 1) * LANES] * piece
                total = total + rmap_ref[j, :, g * LANES : (g + 1) * LANES] * piece
            vw_ref[p, 0, j : j + 1, 0:leaf_size] = vectors[j]
            vw_ref[p, 0, j : j + 1, leaf_size : leaf_size + skel] = row_of(part)
        vw_ref[p, 0, per : per + 1, 0:skel] = row_of(total)
        for k in units:
            start(
                vw_ref.at[p, 0],
                vw_ref.at[p, inverse(k)],
                vw_sem.at[p, 0, k - 1],
                vw_sem.at[p, 1, inverse(k) - 1],
                (t, sub_of(k)),
            )
        start(
            vw_ref.at[p, 0],
            vw_ref.at[p, halo],
            vw_sem.at[p, 0, halo - 1],
            vw_sem.at[p, 1, halo - 1],
            (prev_leaf, s),
        )

    def near_block(r, c, m1, m2):
        va = None
        if m2 is not None:
            va = [
                vrow_ref[c, :, g * LANES : (g + 1) * LANES] * m2
                for g in range(groups)
            ]
        acc = [jnp.zeros((8, LANES), F32) for _ in range(groups)]
        for m in range(0, leaf_size, CHUNK):
            inner = jnp.dot(row_ref[r, m : m + CHUNK], col_ref[c], preferred_element_type=F32)
            e = jnp.exp2(inner)
            w = vb_ref[r, m : m + CHUNK]
            tot = None
            for g in range(groups):
                piece = e[:, g * LANES : (g + 1) * LANES]
                acc[g] = acc[g] + fold(piece * w)
                if va is not None:
                    q = piece * va[g]
                    tot = q if tot is None else tot + q
            if va is not None:
                acc2_ref[r, m : m + CHUNK] += tot
        for g in range(groups):
            acc1_ref[c, :, g * LANES : (g + 1) * LANES] += acc[g] * m1

    def table_row(table, place, slot):
        return table[place, pl.ds(slot, 1), :]

    def own_pair(r, c, k, j, both=True):
        m1 = table_row(ntab_ref, c, cols + s * per + r)
        m2 = table_row(ntab_ref, r, cols + sub_of(k) * per + j) if both else None
        near_block(r, c, m1, m2)

    def near_diagonal():
        def diagonal(i, carry):
            own_pair(i, i, 0, i, False)
            return carry

        lax.fori_loop(0, per, diagonal, 0, unroll=per)

    def near_own():
        for d in range(1, per // 2 + 1):
            count = per if 2 * d < per else per // 2

            def pair(i, carry):
                j = lax.rem(i + d, per)
                own_pair(i, j, 0, j)
                return carry

            lax.fori_loop(0, count, pair, 0, unroll=count)

    def near_unit(k):
        half = per // 2

        def pair(b, carry):
            o = lax.div(b, half)
            j = 2 * lax.rem(b, half) + lax.rem(o + upper(k), 2)
            own_pair(o, k * per + j, k, j)
            return carry

        lax.fori_loop(0, per * half, pair, 0, unroll=per * half)

    def near_halo(first, last):
        def outer(run, carry):
            i, pair = lax.rem(run, per), lax.div(run, per)

            def step(b, carry):
                c = pair * 2 * per + b
                place = sub_of_dynamic(lax.div(c, per)) * per + lax.rem(c, per)
                m1 = table_row(ntab_ref, c, 2 * cols + s * per + i)
                m2 = table_row(ntab_ref, cols + i, place)
                near_block(per + i, c, m1, m2)
                return carry

            return lax.fori_loop(0, 2 * per, step, carry, unroll=2 * per)

        lax.fori_loop(first, last, outer, 0)

    def far_block(p, r, k, parity):
        inner = jnp.dot(zrow_ref[r], zcol_ref[k], preferred_element_type=F32)
        both = parity is not None or r == 1
        for i in range(per):
            acc, ways = [], []
            for j in range(per):
                peer = sub_of(k) * per + j
                slot = (cols if r == 0 else 2 * cols) + s * per + i
                m1 = table_row(ftab_ref, k * per + j, slot)
                m2 = table_row(ftab_ref, i if r == 0 else cols + i, (cols if r == 0 else 0) + peer)
                if parity is not None:
                    use = (1 - lax.rem(parity + i + j, 2)).astype(F32)
                    m1, m2 = m1 * use, m2 * use
                w = vw_ref[p, k, j : j + 1, leaf_size : leaf_size + skel]
                ways.append((m1, w * m2))
            rows = slice(i * skel, (i + 1) * skel)
            e = jnp.exp2(inner[rows])
            wb = wb_ref[r, rows]
            tot = None
            for j in range(per):
                piece = e[:, j * skel : (j + 1) * skel]
                acc.append(fold(piece * wb))
                if both:
                    q = piece * ways[j][1]
                    tot = q if tot is None else tot + q
            if both:
                fac2_ref[r, rows] += tot
            for j in range(per):
                fac1_ref[k, :, j * skel : (j + 1) * skel] += acc[j] * ways[j][0]

    def spread(p, k):
        for j in range(per):
            value = vw_ref[p, k, j : j + 1, 0:leaf_size]
            if k != halo:
                vrow_ref[k * per + j] = value
            if k in (0, halo):
                r = j if k == 0 else per + j
                vb_ref[r] = column_of(value)
                wb_ref[r // per, j * skel : (j + 1) * skel] = column_of(
                    vw_ref[p, k, j : j + 1, leaf_size : leaf_size + skel]
                )

    def wait_vw(p, k):
        arrived(vw_ref.at[p, k], vw_sem.at[p, 0, k - 1], vw_sem.at[p, 1, k - 1])

    def clear():
        acc1_ref[...] = jnp.zeros_like(acc1_ref)
        acc2_ref[...] = jnp.zeros_like(acc2_ref)
        fac1_ref[...] = jnp.zeros_like(fac1_ref)
        fac2_ref[...] = jnp.zeros_like(fac2_ref)

    home = lax.rem(t, subs)

    def send_root_weights(p):
        total = vw_ref[p, 0, per : per + 1, 0:skel]
        for k in units:
            total = total + vw_ref[p, k, per : per + 1, 0:skel]
        wroot_own[p] = jnp.broadcast_to(total, (8, skel))

        @pl.when(s == home)
        def _():
            for d in range(1, leaves):
                copy(
                    wroot_own.at[p],
                    wroot_in.at[p, lax.div(t, subs)],
                    wroot_send.at[p, d - 1],
                    wroot_recv.at[p, lax.div(t, subs)],
                    (lax.rem(t + d, leaves), s),
                ).start()

    def root_of(q):
        return q * subs + s

    def present(q):
        u = root_of(q)
        return jnp.logical_and(u != t, u < leaves)

    def top(p):
        total = jnp.zeros((8, LANES), F32)
        for q in range(quota):

            @pl.when(present(q))
            def _():
                arrived(wroot_in.at[p, q], wroot_send.at[p, 0], wroot_recv.at[p, q])

            @pl.when(jnp.logical_not(present(q)))
            def _():
                wroot_in[p, q] = jnp.zeros((8, skel), F32)

            column = column_of(wroot_in[p, q, 0:1, :])
            total = total + fold(kroot_ref[q] * column)
        return jnp.sum(total, axis=0, keepdims=True)

    def reduce_halo(p):
        for j in range(per):
            rs_out[p, 0, j : j + 1, 0:leaf_size] = row_of(acc2_ref[per + j])
            rs_out[p, 0, j : j + 1, leaf_size : leaf_size + skel] = row_of(
                fac2_ref[1, j * skel : (j + 1) * skel]
            )
        start(
            rs_out.at[p, 0],
            rs_in.at[p, halo - 1],
            rs_sem.at[p, 0, halo - 1],
            rs_sem.at[p, 1, halo - 1],
            (next_leaf, s),
        )

    def reduce_units(p, root_out):
        for k in units:
            for j in range(per):
                c = k * per + j
                rs_out[p, k, j : j + 1, 0:leaf_size] = jnp.sum(acc1_ref[c], axis=0, keepdims=True)
            rs_out[p, k, 0:per, leaf_size : leaf_size + skel] = jnp.concatenate(
                [
                    jnp.sum(fac1_ref[k, :, j * skel : (j + 1) * skel], axis=0, keepdims=True)
                    for j in range(per)
                ],
                axis=0,
            )
            rs_out[p, k, per : per + 1, 0:skel] = root_out
            start(
                rs_out.at[p, k],
                rs_in.at[p, inverse(k) - 1],
                rs_sem.at[p, 0, k - 1],
                rs_sem.at[p, 1, inverse(k) - 1],
                (t, sub_of(k)),
            )

    def reduce_finish(p, root_out):
        nears, fars = [], []
        for j in range(per):
            nears.append(jnp.sum(acc1_ref[j], axis=0, keepdims=True) + row_of(acc2_ref[j]))
            fars.append(
                jnp.sum(fac1_ref[0, :, j * skel : (j + 1) * skel], axis=0, keepdims=True)
                + row_of(fac2_ref[0, j * skel : (j + 1) * skel])
            )
        for k in range(1, subs + 1):
            arrived(rs_in.at[p, k - 1], rs_sem.at[p, 0, k - 1], rs_sem.at[p, 1, k - 1])
            for j in range(per):
                nears[j] = nears[j] + rs_in[p, k - 1, j : j + 1, 0:leaf_size]
                fars[j] = fars[j] + rs_in[p, k - 1, j : j + 1, leaf_size : leaf_size + skel]
            if k < subs:
                root_out = root_out + rs_in[p, k - 1, per : per + 1, 0:skel]
        root_column = column_of(root_out)
        applied = []
        for j in range(per):
            far_column = column_of(fars[j])
            parts = []
            for g in range(groups):
                lanes = slice(g * LANES, (g + 1) * LANES)
                both = lmap_ref[j, :, lanes] * far_column + rmap_ref[j, :, lanes] * root_column
                parts.append(jnp.sum(both, axis=0, keepdims=True))
            applied.append(nears[j] + jnp.concatenate(parts, axis=1))
        return applied

    loads[2].wait()
    loads[3].wait()
    weigh(0, tree)
    for j in range(early, per):
        send_points(j)
    send_units(basis_ref, bas_in, bas_sem)
    spread(0, 0)
    for k in units:
        arrived(ord_in.at[k - 1], ord_sem.at[0, k - 1], ord_sem.at[1, k - 1])
        for j in range(per):
            vrow_ref[k * per + j] = in_tree_order(k, j)
    clear()
    near_diagonal()

    def forward(j):
        for k in across:
            arrived(xin_ref.at[k, j], pts_send.at[k, j], pts_recv.at[k, j])
            start(
                xin_ref.at[k, j],
                xin_ref.at[k + 1, j],
                pts_send.at[k + 1, j],
                pts_recv.at[k + 1, j],
                (t, sub_of(sibling)),
            )

    def take_points(k):
        arrived(meta_in.at[k - 1], meta_sem.at[0, k - 1], meta_sem.at[1, k - 1])
        for j in range(per):
            if k not in across:
                arrived(xin_ref.at[k, j], pts_send.at[k, j], pts_recv.at[k, j])
        for j in range(per):
            build_col(k * per + j, xin_ref[k, j])
            build_tables(k, j)
            build_skeleton(k, j, True, None)

    def take_halo(j):
        arrived(xin_ref.at[halo, j], pts_send.at[halo, j], pts_recv.at[halo, j])
        build_row(per + j, xin_ref[halo, j])
        build_tables(halo, j)
        build_skeleton(halo, j, False, per + j)

    forward(0)
    take_points(sibling)
    near_unit(sibling)
    for j in range(1, early):
        forward(j)
    arrived(meta_in.at[halo - 1], meta_sem.at[0, halo - 1], meta_sem.at[1, halo - 1])
    wait_vw(0, halo)
    spread(0, halo)
    for j in range(early):
        take_halo(j)
    near_halo(0, early)
    for j in range(early, per):
        forward(j)
    for k in units:
        if k != sibling:
            take_points(k)
            near_unit(k)

    root_points = jnp.zeros((4 * feat, skel), F32)
    for k in range(subs):
        for j in range(per):
            base = (sub_of(k) * per + j) * leaf_size
            chosen = one_hot(rskel_ref[...] - base)
            root_points = root_points + jnp.dot(
                col_ref[k * per + j], chosen.astype(BF16), preferred_element_type=F32
            )
    rcol_ref[...] = root_points.astype(BF16)
    root_own[...] = root_points[0:feat] + root_points[2 * feat : 3 * feat]

    @pl.when(s == home)
    def _():
        for d in range(1, leaves):
            copy(
                root_own,
                root_in.at[lax.div(t, subs)],
                root_send.at[d - 1],
                root_recv.at[lax.div(t, subs)],
                (lax.rem(t + d, leaves), s),
            ).start()

    for k in units:
        wait_vw(0, k)
    send_root_weights(0)
    for j in range(early, per):
        take_halo(j)
    near_halo(early, per * chips)

    def far_halo(p):
        for k in range(subs):
            far_block(p, 1, k, None)

    def far_units(p):
        for k in units:
            far_block(p, 0, k, upper(k))

    far_halo(0)
    reduce_halo(0)
    far_units(0)
    for q in range(quota):

        @pl.when(present(q))
        def _():
            arrived(root_in.at[q], root_send.at[0], root_recv.at[q])

        @pl.when(jnp.logical_not(present(q)))
        def _():
            root_in[q] = root_own[...]

        rows = jnp.concatenate(augmented(root_in[q], scale, True), axis=0).T.astype(BF16)
        kroot_ref[q] = jnp.exp2(jnp.dot(rows, rcol_ref[...], preferred_element_type=F32))

    root_out = top(0)
    reduce_units(0, root_out)
    near_own()
    far_block(0, 0, 0, None)
    applied = reduce_finish(0, root_out)
    first = [tree[j] - (applied[j] + RIDGE_SHIFT * tree[j]) / ritz_ref[0] for j in range(per)]

    weigh(1, first)
    spread(1, 0)
    clear()
    near_diagonal()
    wait_vw(1, sibling)
    spread(1, sibling)
    near_unit(sibling)
    others = [k for k in units if k != sibling]
    for k in others:
        wait_vw(1, k)
        spread(1, k)
    wait_vw(1, halo)
    spread(1, halo)
    send_root_weights(1)
    near_halo(0, per * chips)
    far_halo(1)
    reduce_halo(1)
    for k in others:
        near_unit(k)
    far_units(1)
    root_out = top(1)
    reduce_units(1, root_out)
    near_own()
    far_block(1, 0, 0, None)
    applied = reduce_finish(1, root_out)
    square = jnp.zeros((1, leaf_size), F32)
    placed = jnp.zeros((rows_all, LANES), F32)
    for j in range(per):
        v0 = vw_ref[0, 0, j : j + 1, 0:leaf_size]
        v1 = vw_ref[1, 0, j : j + 1, 0:leaf_size]
        second = v1 - (applied[j] + RIDGE_SHIFT * v1) / ritz_ref[1]
        grown = v0 - second
        square = square + grown * grown
        in_row, in_lane = hot_rows(order_of(0, j))
        held = jnp.concatenate(split3(jnp.where(in_row, grown, 0.0)), axis=0)
        hot = jnp.where(in_lane, 1.0, 0.0).astype(BF16)
        spots = lax.dot_general(
            held.astype(BF16), hot, (((1,), (1,)), ((), ())), preferred_element_type=F32
        )
        placed = placed + (
            spots[0:rows_all] + spots[rows_all : 2 * rows_all] + spots[2 * rows_all : 3 * rows_all]
        )
    placed_ref[...] = placed.reshape(subs, rows_own, LANES)
    for k in units:
        start(
            placed_ref.at[sub_of(k)],
            fin_in.at[inverse(k) - 1],
            fin_sem.at[0, k - 1],
            fin_sem.at[1, inverse(k) - 1],
            (t, sub_of(k)),
        )

    part = jnp.zeros((basis_count, LANES), F32)
    for k in range(subs):
        if k:
            arrived(bas_in.at[k - 1], bas_sem.at[0, k - 1], bas_sem.at[1, k - 1])
        spots = placed_ref[sub_of(k)]
        for r in range(rows_own):
            lanes = slice(r * LANES, (r + 1) * LANES)
            piece = basis_ref[:, lanes] if k == 0 else bas_in[k - 1, :, lanes]
            part = part + piece * spots[r : r + 1]
    corner = jnp.logical_and(lane_small == 1 + basis_count, sub_small == 0)
    tot_own[...] = (
        gram_ref[...]
        + jnp.where(lane_small == 0, jnp.sum(part, axis=1, keepdims=True), 0.0)
        + jnp.where(corner, jnp.sum(square, axis=1, keepdims=True), 0.0)
    )
    send_units(tot_own, tot_in, tots_sem)
    for k in units:
        arrived(tot_in.at[k - 1], tots_sem.at[0, k - 1], tots_sem.at[1, k - 1])
    tot_all[0] = tot_own[...]
    for k in units:
        tot_all[k] = tot_in[k - 1]
    total = tot_all[sub_order(chip, core, 0, chips)]
    for i in range(1, subs):
        total = total + tot_all[sub_order(chip, core, i, chips)]
    tot_sub[t] = total
    for d in range(1, leaves):
        start(
            tot_sub.at[t],
            tot_sub.at[t],
            totl_sem.at[0, d - 1],
            totl_sem.at[1, d - 1],
            (lax.rem(t + d, leaves), s),
        )
    user = placed_ref[s]
    for k in units:
        arrived(fin_in.at[k - 1], fin_sem.at[0, k - 1], fin_sem.at[1, k - 1])
        user = user + fin_in[k - 1]
    for d in range(1, leaves):
        slot = tot_sub.at[lax.rem(t + leaves - d, leaves)]
        arrived(slot, totl_sem.at[0, d - 1], totl_sem.at[1, d - 1])
    total = tot_sub[0]
    for u in range(1, leaves):
        total = total + tot_sub[u]
    proj = total[:, 0:1]
    squares = jnp.sum(jnp.where(corner, total, 0.0), keepdims=True)
    proj_row = jnp.sum(jnp.where(lane_small == 1 + sub_small, proj, 0.0), axis=0, keepdims=True)
    gram_proj = jnp.sum(
        jnp.where(jnp.logical_and(lane_small >= 1, lane_small <= basis_count), total, 0.0) * proj_row,
        axis=1,
        keepdims=True,
    )
    length_sq = (
        squares
        - 2.0 * jnp.sum(proj * proj, axis=0, keepdims=True)
        + jnp.sum(proj * gram_proj, axis=0, keepdims=True)
    )
    norm = jnp.sqrt(length_sq + EPSILON)
    hess = jnp.sum(jnp.where(lane_small == sub_small, proj, 0.0), axis=0, keepdims=True)
    hess_ref[...] = hess + jnp.where(lane_small[0:1] == basis_count, norm, 0.0)
    for r in range(rows_own):
        span = jnp.sum(basis_ref[:, r * LANES : (r + 1) * LANES] * proj, axis=0, keepdims=True)
        orth_ref[r : r + 1] = user[r : r + 1] - span

    for c in started:
        c.wait_send()

    @pl.when(s == home)
    def _():
        there = (next_leaf, s)
        for d in range(1, leaves):
            q = lax.div(t, subs)
            copy(root_own, root_in.at[q], root_send.at[d - 1], root_recv.at[q], there).wait_send()
            for p in range(2):
                copy(
                    wroot_own.at[p], wroot_in.at[p, q], wroot_send.at[p, d - 1], wroot_recv.at[p, q], there
                ).wait_send()


def sub_order(chip, core, i, chips):
    return lax.rem(i // 2 + chips - chip, chips) * 2 + lax.rem(i % 2 + 2 - core, 2)


def shards(
    points,
    leaf_maps,
    root_maps,
    current,
    krylov_basis,
    ritz_roots,
    point_order,
    skeleton,
    root_skeleton,
    near_list,
    far_list,
):
    per, skel, leaf_size = leaf_maps.shape
    feat = points.shape[1]
    subs, leaves = lax.axis_size("sub"), lax.axis_size("leaf")
    near_count, far_count = near_list.shape[1], far_list.shape[1]
    basis_count = krylov_basis.shape[0]
    dims = (per, leaf_size, feat, skel, leaves, subs, near_count, far_count, basis_count)
    cols, rows_own = per * subs, per * leaf_size // LANES
    quota = -(-leaves // subs)
    wide = leaf_size + skel
    dma = pltpu.SemaphoreType.DMA
    scratch = [
        pltpu.VMEM((per * leaf_size, feat), F32),
        pltpu.VMEM((per, feat, leaf_size), F32),
        pltpu.VMEM((per, skel, leaf_size), F32),
        pltpu.VMEM((per, skel, leaf_size), F32),
        pltpu.VMEM((basis_count, rows_own * LANES), F32),
        pltpu.VMEM((subs + 1, per, feat, leaf_size), F32),
        pltpu.VMEM((per, leaf_size), F32),
        pltpu.VMEM((subs, per, leaf_size), F32),
        pltpu.VMEM((subs - 1, rows_own, LANES), F32),
        pltpu.VMEM((subs - 1, rows_own, LANES), jnp.int32),
        pltpu.VMEM((subs - 1, basis_count, rows_own * LANES), F32),
        pltpu.VMEM((cols, 4 * feat, leaf_size), BF16),
        pltpu.VMEM((2 * per, leaf_size, 4 * feat), BF16),
        pltpu.VMEM((subs, 4 * feat, per * skel), BF16),
        pltpu.VMEM((2, per * skel, 4 * feat), BF16),
        pltpu.VMEM((cols + per, 3 * cols, LANES), F32),
        pltpu.VMEM((cols + per, 3 * cols, LANES), F32),
        pltpu.VMEM((2, subs + 1, 2 * per, wide), F32),
        pltpu.VMEM((cols, 1, leaf_size), F32),
        pltpu.VMEM((2 * per, leaf_size, LANES), F32),
        pltpu.VMEM((2, per * skel, LANES), F32),
        pltpu.VMEM((cols, 8, leaf_size), F32),
        pltpu.VMEM((2 * per, leaf_size, LANES), F32),
        pltpu.VMEM((subs, 8, per * skel), F32),
        pltpu.VMEM((2, per * skel, LANES), F32),
        pltpu.VMEM((feat, skel), F32),
        pltpu.VMEM((quota, feat, skel), F32),
        pltpu.VMEM((4 * feat, skel), BF16),
        pltpu.VMEM((quota, skel, LANES), F32),
        pltpu.VMEM((2, 8, skel), F32),
        pltpu.VMEM((2, quota, 8, skel), F32),
        pltpu.VMEM((2, subs, 2 * per, wide), F32),
        pltpu.VMEM((2, subs, 2 * per, wide), F32),
        pltpu.VMEM((subs, rows_own, LANES), F32),
        pltpu.VMEM((subs - 1, rows_own, LANES), F32),
        pltpu.VMEM((basis_count, LANES), F32),
        pltpu.VMEM((subs - 1, basis_count, LANES), F32),
        pltpu.VMEM((leaves, basis_count, LANES), F32),
        pltpu.VMEM((subs, basis_count, LANES), F32),
        pltpu.VMEM((basis_count, LANES), F32),
        dma((4,)),
        dma((2, subs - 1)),
        dma((2, subs - 1)),
        dma((2, subs - 1)),
        dma((2, subs)),
        dma((subs + 1, per)),
        dma((subs + 1, per)),
        dma((2, 2, subs)),
        dma((2, 2, subs)),
        dma((leaves - 1,)),
        dma((quota,)),
        dma((2, leaves - 1)),
        dma((2, quota)),
        dma((2, subs - 1)),
        dma((2, subs - 1)),
        dma((2, leaves - 1)),
    ]
    orth, hess = pl.pallas_call(
        lambda *refs: kernel_body(dims, *refs),
        out_shape=[
            jax.ShapeDtypeStruct((rows_own, LANES), F32),
            jax.ShapeDtypeStruct((1, LANES), F32),
        ],
        in_specs=[ANY] * 3 + [VMEM] * 6 + [ANY, SMEM],
        out_specs=[VMEM] * 2,
        scratch_shapes=scratch,
        compiler_params=pltpu.CompilerParams(
            collective_id=0, has_side_effects=True, vmem_limit_bytes=48 * 1024 * 1024
        ),
        name="step",
    )(
        points,
        leaf_maps,
        root_maps,
        current.reshape(rows_own, LANES),
        point_order.reshape(rows_own, LANES),
        skeleton,
        root_skeleton,
        near_list,
        far_list,
        krylov_basis,
        ritz_roots,
    )
    return orth.reshape(-1), hess[0, : basis_count + 1]


def solution(mesh):
    return jax.shard_map(
        shards,
        mesh=mesh,
        in_specs=(
            P(("leaf", "sub"), None),
            P(("leaf", "sub"), None, None),
            P(("leaf", "sub"), None, None),
            P(("leaf", "sub")),
            P(None, ("leaf", "sub")),
            P(),
            P(("leaf", "sub")),
            P(("leaf", "sub"), None),
            P("leaf", None),
            P(("leaf", "sub"), None),
            P(("leaf", "sub"), None),
        ),
        out_specs=(P(("leaf", "sub")), P()),
        check_vma=False,
    )
```
